256 devices in a mesh: group: 4 (over y), resp: 16 (over z, core), tp: 4 (over x).
Axes of the slice: x: 4, y: 4, z: 8, core: 2. Of those that a mesh axis runs over, the one named last changes fastest.
Arguments:
- query: bfloat16 [16384, 4096], P(('group', 'resp'), 'tp'), parts along dimension 0, may hold values from -150 to 150
- resp_kv: bfloat16 [16384, 2, 1024], P(('group', 'resp'), None, 'tp'), parts along dimension 0, may hold values from -6 to 6
- prefix_kv: bfloat16 [4096, 2, 1024], P(('group', 'resp'), None, 'tp'), parts along dimension 0, may hold values from -6 to 6
- ssm_x: bfloat16 [16384, 8192], P(('group', 'resp'), 'tp'), parts along dimension 0, may hold values from -6 to 6
- bc: bfloat16 [16384, 2, 256], P(('group', 'resp')), parts along dimension 0, may hold values from -1.5 to 1.5
- step_size: float32 [256, 4096], P(('group', 'tp'), 'resp'), parts along dimension 0, may hold values from 0 to 1
- prefix_state: float32 [64, 64, 128, 256], P(('group', 'resp'), 'tp'), parts along dimension 0, may hold values from -1.5 to 1.5
- owner: int32 [256], P(('group', 'tp')), parts along dimension 0, may hold values from 0 to 15
- lengths: int32 [64], P(('group', 'resp')), parts along dimension 0, may hold values from 64 to 256, as said below
- advantage: float32 [64], P(('group', 'resp')), parts along dimension 0, may hold values from -3 to 3
- grad_attn: bfloat16 [16384, 4096], P(('group', 'resp'), 'tp'), parts along dimension 0, may hold values from -6 to 6
- grad_ssm: bfloat16 [16384, 8192], P(('group', 'resp'), 'tp'), parts along dimension 0, may hold values from -6 to 6
Outputs:
- attn_out: bfloat16 [16384, 4096], P(('group', 'resp'), 'tp'), parts along dimension 0
- ssm_out: bfloat16 [16384, 8192], P(('group', 'resp'), 'tp'), parts along dimension 0
- grad_query: bfloat16 [16384, 4096], P(('group', 'resp'), 'tp'), parts along dimension 0
- grad_prefix_kv: bfloat16 [4096, 2, 1024], P(('group', 'resp'), None, 'tp'), parts along dimension 0
- grad_bc: bfloat16 [16384, 2, 256], P(('group', 'resp', 'tp')), parts along dimension 0
- grad_state: float32 [256, 128, 256], P(('group', 'tp')), parts along dimension 0
The draws below stay inside these ranges and needn't reach their ends.
There are 4 independent parts, one for each index of `group`. The reference program is written for one: setup_inputs(seed, part) draws one part's arguments, and reference() takes and returns one part's arrays. A program takes and returns all parts, laid end to end along the dimension named above; each array names one. Nothing has to cross between parts.
Inputs may be any that keep to these rules, and one draw needn't show every extreme that they name: `lengths`: one response of each group has exactly 256 live tokens.
All inputs are finite; a program needn't handle non-finite values.
Results may differ from the reference program's by a relative error of at most 0.025.
Values may be sent and summed in bfloat16 or wider, within the bound.
No kernel may reach another device: no remote copies, remote signals or barrier semaphores. Data moves between devices by JAX's collectives and lax.ppermute only.
A program may use at most 128 MiB of HBM per device.

```python
import math
import jax
import jax.numpy as jnp
from jax import lax

Q_HEADS = 32
KV_HEADS = 8
HEAD_DIM = 128
STATE_SPACE_HEAD = 64
SSM_DIM = 128
STATE_DIM = 256
L_RESP = 256
RESPONSE_TOKENS = 4096
PREFIX_LEN = 1024
N_RESP = 16


def prefix_rows(key):
    base_rows = jnp.clip(jax.random.normal(jax.random.fold_in(key, 11), (PREFIX_LEN, 2, KV_HEADS * HEAD_DIM), jnp.float32), -5.0, 5.0)
    return base_rows


def draw_prefix_kv(key, part):
    return prefix_rows(key).astype(jnp.bfloat16)


def draw_query(key, part):
    drawn_rows = jnp.clip(jax.random.normal(jax.random.fold_in(key, 13), (RESPONSE_TOKENS, Q_HEADS * HEAD_DIM), jnp.float32), -5.0, 5.0)
    return drawn_rows.astype(jnp.bfloat16)


def draw_step_size(key, part):
    rate_low = 0.02 / L_RESP
    rate_high = 0.03
    baseline_rate = jnp.exp(jax.random.uniform(jax.random.fold_in(key, 21), (STATE_SPACE_HEAD, 1), jnp.float32, math.log(rate_low), math.log(rate_high)))
    per_response = jnp.exp(jax.random.uniform(jax.random.fold_in(key, 22), (RESPONSE_TOKENS // L_RESP,), jnp.float32, math.log(0.5), math.log(2.0)))
    response_multiplier = jnp.repeat(per_response, L_RESP)[None, :]
    jaggedness_level = jax.random.uniform(jax.random.fold_in(key, 23), (STATE_SPACE_HEAD, RESPONSE_TOKENS), jnp.float32, 0.5, 1.5)
    spike_location = (jax.random.randint(jax.random.fold_in(key, 24), (1, RESPONSE_TOKENS), 0, 96) == 0).astype(jnp.float32)
    spike_extent = jax.random.uniform(jax.random.fold_in(key, 25), (STATE_SPACE_HEAD, RESPONSE_TOKENS), jnp.float32, 0.2, 0.7)
    return baseline_rate * response_multiplier * jaggedness_level + spike_location * spike_extent


def draw_lengths(key, part):
    count = RESPONSE_TOKENS // L_RESP
    drawn = jax.random.randint(jax.random.fold_in(key, 31), (count,), L_RESP // 4, L_RESP + 1)
    longest = jax.random.randint(jax.random.fold_in(key, 32), (), 0, count)
    return jnp.where(jnp.arange(count) == longest, L_RESP, drawn).astype(jnp.int32)


def plant(result, rng, low, largest):
    spot = [jax.random.randint(jax.random.fold_in(rng, axis), (), 0, length) for axis, length in enumerate(result.shape)]
    widest = result.shape.index(max(result.shape))
    next_to = spot[:widest] + [(spot[widest] + 1) % result.shape[widest]] + spot[widest + 1:]
    return result.at[tuple(spot)].set(low).at[tuple(next_to)].set(largest)


def levels(stream_key, extent, cuts, low, high):
    gain = 1.0
    for position, shards_of in cuts:
        heights = jax.random.uniform(jax.random.fold_in(jax.random.fold_in(stream_key, 6), position), (shards_of,), jnp.float32, low / len(cuts), high / len(cuts))
        gain = gain * jnp.repeat(jnp.exp(heights), extent[position] // shards_of).reshape((-1,) + (1,) * (len(extent) - 1 - position))
    return gain


def centred(rng, dims, deviation, limit, shards=(), held_as=jnp.bfloat16):
    values = deviation * jax.random.normal(rng, dims, jnp.float32)
    if shards:
        values = values * levels(rng, dims, shards, -0.22, 0.18)
    return jnp.clip(values, -limit, limit).astype(held_as)


def setup_inputs(seed: int = 0, part: int = 0) -> dict:
    splits = jax.random.split(jax.random.key(seed), 13)
    part_keys = jax.random.split(jax.random.fold_in(splits[12], part), 13)
    return {
        "query": draw_query(jax.random.fold_in(jax.random.fold_in(splits[12], part), 71), part),
        "resp_kv": centred(part_keys[1], (RESPONSE_TOKENS, 2, KV_HEADS * HEAD_DIM), 1.0, 6.0, ((0, 16), (2, 4))),
        "prefix_kv": draw_prefix_kv(jax.random.fold_in(jax.random.fold_in(splits[12], part), 71), part),
        "ssm_x": centred(part_keys[3], (RESPONSE_TOKENS, STATE_SPACE_HEAD * SSM_DIM), 1.0, 6.0, ((0, 16), (1, 4))),
        "bc": centred(part_keys[4], (RESPONSE_TOKENS, 2, STATE_DIM), 0.25, 1.5, ((0, 16),)),
        "step_size": draw_step_size(jax.random.fold_in(jax.random.fold_in(splits[12], part), 71), part),
        "prefix_state": centred(part_keys[6], (N_RESP, STATE_SPACE_HEAD, SSM_DIM, STATE_DIM), 0.25, 1.5, ((0, 16), (1, 4)), jnp.float32),
        "owner": plant(jax.random.randint(part_keys[7], (STATE_SPACE_HEAD,), 0, N_RESP), jax.random.fold_in(part_keys[7], 1), 0, N_RESP - 1).astype(jnp.int32),
        "lengths": draw_lengths(jax.random.fold_in(jax.random.fold_in(splits[12], part), 71), part),
        "advantage": centred(part_keys[9], (N_RESP,), 1.0, 3.0, ((0, 16),), jnp.float32),
        "grad_attn": centred(part_keys[10], (RESPONSE_TOKENS, Q_HEADS * HEAD_DIM), 1.0, 6.0, ((0, 16), (1, 4))),
        "grad_ssm": centred(part_keys[11], (RESPONSE_TOKENS, STATE_SPACE_HEAD * SSM_DIM), 1.0, 6.0, ((0, 16), (1, 4))),
    }


highest = lax.Precision.HIGHEST

def attention_part(query_rows, own_kv, prefix_kv, grad_out):
    steps_len = query_rows.shape[0]
    group_size = Q_HEADS // KV_HEADS
    inv_scale = 1.0 / math.sqrt(HEAD_DIM)
    query_heads = query_rows.astype(jnp.float32).reshape(steps_len, KV_HEADS, group_size, HEAD_DIM)
    grad_heads = grad_out.astype(jnp.float32).reshape(steps_len, KV_HEADS, group_size, HEAD_DIM)
    prefix_keys = prefix_kv[:, 0].astype(jnp.float32).reshape(PREFIX_LEN, KV_HEADS, HEAD_DIM)
    prefix_values = prefix_kv[:, 1].astype(jnp.float32).reshape(PREFIX_LEN, KV_HEADS, HEAD_DIM)
    own_keys = own_kv[:, 0].astype(jnp.float32).reshape(steps_len, KV_HEADS, HEAD_DIM)
    own_values = own_kv[:, 1].astype(jnp.float32).reshape(steps_len, KV_HEADS, HEAD_DIM)
    positions = jnp.arange(steps_len)
    causal = positions[None, :] <= positions[:, None]
    prefix_scores = jnp.einsum('tgid,kgd->gitk', query_heads, prefix_keys) * inv_scale
    own_scores = jnp.where(causal, jnp.einsum('tgid,kgd->gitk', query_heads, own_keys) * inv_scale, -jnp.inf)
    row_top = jnp.maximum(lax.optimization_barrier(jnp.max(prefix_scores, -1)), lax.optimization_barrier(jnp.max(own_scores, -1)))
    row_total = lax.optimization_barrier(jnp.sum(jnp.exp(prefix_scores - row_top[..., None]), -1)) + lax.optimization_barrier(jnp.sum(jnp.exp(own_scores - row_top[..., None]), -1))
    log_total = row_top + jnp.log(row_total)
    prefix_weights = jnp.exp(prefix_scores - log_total[..., None]).astype(jnp.bfloat16).astype(jnp.float32)
    own_weights = jnp.exp(own_scores - log_total[..., None]).astype(jnp.bfloat16).astype(jnp.float32)
    attended = jnp.einsum('gitk,kgd->tgid', prefix_weights, prefix_values) + jnp.einsum('gitk,kgd->tgid', own_weights, own_values)
    attn_out = attended.reshape(steps_len, -1).astype(jnp.bfloat16)
    row_delta = jnp.transpose(lax.optimization_barrier(jnp.sum(grad_heads * attended, -1)), (1, 2, 0))
    prefix_slope = jnp.einsum('tgid,kgd->gitk', grad_heads, prefix_values)
    own_slope = jnp.einsum('tgid,kgd->gitk', grad_heads, own_values)
    prefix_score_grad = (prefix_weights * (prefix_slope - row_delta[..., None]) * inv_scale).astype(jnp.bfloat16).astype(jnp.float32)
    own_score_grad = (own_weights * (own_slope - row_delta[..., None]) * inv_scale).astype(jnp.bfloat16).astype(jnp.float32)
    grad_query = (jnp.einsum('gitk,kgd->tgid', prefix_score_grad, prefix_keys) + jnp.einsum('gitk,kgd->tgid', own_score_grad, own_keys)).reshape(steps_len, -1).astype(jnp.bfloat16)
    grad_keys = jnp.einsum('gitk,tgid->kgd', prefix_score_grad, query_heads)
    grad_values = jnp.einsum('gitk,tgid->kgd', prefix_weights, grad_heads)
    kv_term = jnp.stack([grad_keys.reshape(PREFIX_LEN, -1), grad_values.reshape(PREFIX_LEN, -1)], axis=1)
    return (attn_out, grad_query, kv_term)

def ssm_part(input_rows, bc_rows, rates, start_state, grad_y):
    steps_len = input_rows.shape[0]
    head_inputs = input_rows.astype(jnp.float32).reshape(steps_len, STATE_SPACE_HEAD, SSM_DIM)
    input_maps = bc_rows[:, 0].astype(jnp.float32)
    read_maps = bc_rows[:, 1].astype(jnp.float32)
    cumulative = jnp.cumsum(rates, axis=1)
    positions = jnp.arange(steps_len)
    causal = positions[None, :] <= positions[:, None]
    segment = jnp.exp(jnp.where(causal[None], cumulative[:, None, :] - cumulative[:, :, None], -jnp.inf))
    pair_inner = jnp.dot(bc_rows[:, 1], bc_rows[:, 0].T, preferred_element_type=jnp.float32)
    mixing = (segment * rates[:, None, :] * pair_inner[None]).astype(jnp.bfloat16).astype(jnp.float32)
    from_inputs = jnp.einsum('hts,shp->thp', mixing, head_inputs)
    carried = jnp.exp(-cumulative)
    from_state = jnp.einsum('tn,hpn->thp', read_maps, start_state, precision=highest) * carried.T[:, :, None]
    ssm_out = (from_inputs + from_state).reshape(steps_len, -1).astype(jnp.bfloat16)
    grad_heads_y = grad_y.astype(jnp.float32).reshape(steps_len, STATE_SPACE_HEAD, SSM_DIM)
    inner_grad = jnp.einsum('thp,shp->hts', grad_heads_y, head_inputs)
    grad_mix = (segment * rates[:, None, :] * inner_grad).astype(jnp.bfloat16).astype(jnp.float32)
    weighted = grad_heads_y * carried.T[:, :, None]
    grad_read = jnp.einsum('hts,sn->tn', grad_mix, input_maps) + jnp.einsum('thp,hpn->tn', weighted, start_state, precision=highest)
    grad_input = jnp.einsum('hts,tn->sn', grad_mix, read_maps)
    state_term = jnp.einsum('thp,tn->hpn', weighted, read_maps, precision=highest)
    grad_bc = jnp.stack([grad_input, grad_read], axis=1).astype(jnp.bfloat16)
    return (ssm_out, grad_bc, state_term)

def reference(query, resp_kv, prefix_kv, ssm_x, bc, step_size, prefix_state, owner, lengths, advantage, grad_attn, grad_ssm):
    slot_hit = (owner[None, :] == jnp.arange(N_RESP, dtype=jnp.int32)[:, None]).astype(prefix_state.dtype)
    start_state = lax.optimization_barrier(jnp.sum(prefix_state * slot_hit[:, :, None, None], axis=0))

    def one_response(carry, index):
        start = (index * L_RESP).astype(jnp.int32)
        query_rows = lax.dynamic_slice_in_dim(query, start, L_RESP, 0)
        own_kv = lax.dynamic_slice_in_dim(resp_kv, start, L_RESP, 0)
        input_rows = lax.dynamic_slice_in_dim(ssm_x, start, L_RESP, 0)
        bc_rows = lax.dynamic_slice_in_dim(bc, start, L_RESP, 0)
        rates = lax.dynamic_slice_in_dim(step_size, start, L_RESP, 1)
        attn_grad_rows = lax.dynamic_slice_in_dim(grad_attn, start, L_RESP, 0)
        ssm_grad_rows = lax.dynamic_slice_in_dim(grad_ssm, start, L_RESP, 0)
        length = lengths[index]
        factor = advantage[index] * L_RESP / length.astype(jnp.float32)
        alive_rows = (jnp.arange(L_RESP) < length).astype(jnp.float32) * factor
        grad_out = (alive_rows[:, None] * attn_grad_rows.astype(jnp.float32)).astype(jnp.bfloat16)
        grad_y = (alive_rows[:, None] * ssm_grad_rows.astype(jnp.float32)).astype(jnp.bfloat16)
        attn_out, grad_query, kv_term = attention_part(query_rows, own_kv, prefix_kv, grad_out)
        ssm_out, grad_bc, state_term = ssm_part(input_rows, bc_rows, rates, start_state, grad_y)
        return ((carry[0] + kv_term, carry[1] + state_term), (attn_out, ssm_out, grad_query, grad_bc))
    initial = (jnp.zeros((PREFIX_LEN, 2, KV_HEADS * HEAD_DIM), jnp.float32), jnp.zeros((STATE_SPACE_HEAD, SSM_DIM, STATE_DIM), jnp.float32))
    totals, stacked = lax.scan(one_response, initial, jnp.arange(N_RESP, dtype=jnp.int32))
    attn_out = stacked[0].reshape(RESPONSE_TOKENS, -1)
    ssm_out = stacked[1].reshape(RESPONSE_TOKENS, -1)
    grad_query = stacked[2].reshape(RESPONSE_TOKENS, -1)
    grad_bc = stacked[3].reshape(RESPONSE_TOKENS, 2, STATE_DIM)
    return (attn_out, ssm_out, grad_query, totals[0].astype(jnp.bfloat16), grad_bc, totals[1])
```

```python
import math

import jax
import jax.numpy as jnp
from jax import lax
from jax.experimental import pallas as pl
from jax.experimental.pallas import tpu as pltpu
from jax.sharding import PartitionSpec as P

D = 128
N = 256
T = 256
CHIPS = 8
KV = 2
GROUP = 4
HEADS = 16
BLK = 64
SCALE = 1.0 / math.sqrt(D)
LOG2E = math.log2(math.e)
f32 = jnp.float32
bf16 = jnp.bfloat16
VMEM = pl.BlockSpec(memory_space=pltpu.VMEM)
SMEM = pl.BlockSpec(memory_space=pltpu.SMEM)


def nn(a, b):
    return lax.dot_general(a, b, (((1,), (0,)), ((), ())), preferred_element_type=f32)


def nt(a, b):
    return lax.dot_general(a, b, (((1,), (1,)), ((), ())), preferred_element_type=f32)


def tn(a, b):
    return lax.dot_general(a, b, (((0,), (0,)), ((), ())), preferred_element_type=f32)


def exact_nn(a, b):
    return lax.dot_general(
        a, b, (((1,), (0,)), ((), ())), preferred_element_type=f32, precision=lax.Precision.HIGHEST
    )


def call(body, outs, n_in, scalars=(), scratch=(), mib=40):
    single = not isinstance(outs, (list, tuple))
    return pl.pallas_call(
        body,
        out_shape=outs,
        in_specs=[SMEM if i in scalars else VMEM for i in range(n_in)],
        out_specs=VMEM if single else [VMEM] * len(outs),
        scratch_shapes=list(scratch),
        compiler_params=pltpu.CompilerParams(vmem_limit_bytes=mib << 20),
    )


def sds(shape, dtype=bf16):
    return jax.ShapeDtypeStruct(shape, dtype)


def to_pair(x):
    return lax.ppermute(x, "resp", [(i, i ^ 1) for i in range(2 * CHIPS)])


def along(x, k):
    pairs = []
    for z in range(CHIPS):
        pairs.append((2 * z, 2 * ((z + k) % CHIPS)))
        pairs.append((2 * z + 1, 2 * ((z - k) % CHIPS) + 1))
    return lax.ppermute(x, "resp", pairs)


def mine(me, j):
    z, c = me // 2, me % 2
    back = 1 - 2 * c
    if j < 6:
        chip = lax.rem(z - (j // 2 + 1) * back + CHIPS, CHIPS)
        return 2 * chip + (c if j % 2 == 0 else 1 - c)
    if j == 6:
        return 2 * lax.rem(z + 4, CHIPS) + c
    return me


def gather(own, both):
    got = [along(both, k) for k in (1, 2, 3)] + [along(own, 4)]
    return got, [to_pair(g) for g in got]


def pair_add_kernel(b, ours_ref, theirs_ref, u1, u2, u3, u4, own):
    for i, u in enumerate((u1, u2, u3)):
        rows = pl.ds(2 * b * i, 2 * b)
        u[...] = (ours_ref[rows].astype(f32) + theirs_ref[rows].astype(f32)).astype(bf16)
    rows = pl.ds(6 * b, b)
    u4[...] = (ours_ref[rows].astype(f32) + theirs_ref[rows].astype(f32)).astype(bf16)
    rows = pl.ds(7 * b, b)
    own[...] = ours_ref[rows].astype(f32) + theirs_ref[rows].astype(f32)


def ring_add_kernel(b, own_ref, v1, v2, v3, v4, out_ref):
    total = own_ref[...] + v4[...].astype(f32)
    rest = None
    for v in (v1, v2, v3):
        total = total + v[:b].astype(f32)
        rest = v[b:].astype(f32) if rest is None else rest + v[b:].astype(f32)
    out_ref[:b] = total.astype(bf16)
    out_ref[b:] = rest.astype(bf16)


def scatter(ours, theirs):
    b, width = ours.shape[0] // 8, ours.shape[1]
    got = to_pair(theirs)
    u1, u2, u3, u4, own = call(
        lambda *refs: pair_add_kernel(b, *refs),
        [sds((2 * b, width))] * 3 + [sds((b, width)), sds((b, width), f32)],
        2,
    )(ours, got)
    v = [along(u, -k) for k, u in ((1, u1), (2, u2), (3, u3), (4, u4))]
    return call(lambda *refs: ring_add_kernel(b, *refs), sds((2 * b, width)), 5)(own, *v)


def cross_add_kernel(b, a_ref, w_ref, out_ref):
    out_ref[:b] = (a_ref[:b].astype(f32) + w_ref[b:].astype(f32)).astype(bf16)
    out_ref[b:] = (a_ref[b:].astype(f32) + w_ref[:b].astype(f32)).astype(bf16)


def alive_rows(len_ref, adv_ref, width):
    length = len_ref[0]
    factor = adv_ref[0] * (T / length.astype(f32))
    rows = lax.broadcasted_iota(jnp.int32, (T, width), 0)
    return jnp.where(rows < length, factor, 0.0)


def live(alive, grad):
    return (alive * grad.astype(f32)).astype(bf16)


def cumulate(step):
    s = lax.broadcasted_iota(jnp.int32, (T, T), 0)
    t = lax.broadcasted_iota(jnp.int32, (T, T), 1)
    return exact_nn(step, (s <= t).astype(f32))


def down(row, width):
    return jnp.transpose(jnp.broadcast_to(row, (width, T)))


def prep_kernel(me_ref, len_ref, adv_ref, owner_ref, gy_ref, step_ref, bc_ref, state_ref, ours_ref, theirs_ref, car):
    me = me_ref[0]
    alive = alive_rows(len_ref, adv_ref, D)
    car[...] = jnp.exp(-cumulate(step_ref[...]))
    read = bc_ref[:, N:]
    for side, out in ((me, ours_ref), (me + 1 - 2 * lax.rem(me, 2), theirs_ref)):
        for j in range(8):
            h = mine(side, j)
            cols = pl.ds(pl.multiple_of(h * D, D), D)
            held = jnp.where(owner_ref[h] == me, 1.0, 0.0)
            out[2 * D * j : 2 * D * j + D] = jnp.where(held > 0.5, state_ref[0, h], 0.0).astype(bf16)
            weighted = live(alive, gy_ref[:, cols]).astype(f32) * down(car[pl.ds(h, 1)], D)
            out[2 * D * j + D : 2 * D * (j + 1)] = tn(weighted.astype(bf16), read).astype(bf16)


def ssm_local_kernel(len_ref, adv_ref, x_ref, gy_ref, step_ref, bc_ref, part_ref, gsum_ref):
    alive = alive_rows(len_ref, adv_ref, D)
    step = step_ref[...]
    cum = cumulate(step)
    read, inp = bc_ref[:, N:], bc_ref[:, :N]
    t = lax.broadcasted_iota(jnp.int32, (T, T), 0)
    s = lax.broadcasted_iota(jnp.int32, (T, T), 1)
    causal = s <= t
    inner = nt(read, inp)
    for h in range(HEADS):
        cols = slice(h * D, h * D + D)
        row = cum[h : h + 1]
        seg = jnp.exp(jnp.where(causal, row - down(row, T), -jnp.inf)) * step[h : h + 1]
        x = x_ref[:, cols]
        gy = live(alive, gy_ref[:, cols])
        part_ref[:, cols] = nn((seg * inner).astype(bf16), x)
        mix = (seg * nt(gy, x)).astype(bf16).astype(f32)
        if h == 0:
            gsum_ref[...] = mix
        else:
            gsum_ref[...] += mix


def split2(a):
    hi = a.astype(bf16)
    return hi, (a - hi.astype(f32)).astype(bf16)


def ssm_state_kernel(
    me_ref, tp_ref, len_ref, adv_ref, gy_ref, step_ref, bc_ref, part_ref, gsum_ref,
    both, r1, r2, r3, r4, s1, s2, s3, s4,
    out_ref, state_out, g0, g1, g2, g3, car, acc, maps,
):
    me = me_ref[0]
    alive = alive_rows(len_ref, adv_ref, D)
    car[...] = jnp.exp(-cumulate(step_ref[...]))
    read, inp = bc_ref[:, N:], bc_ref[:, :N]
    hi, lo = split2(gsum_ref[...])
    acc[...] = nn(hi, inp) + nn(lo, inp)
    maps[:, :N] = tn(hi, read) + tn(lo, read)
    twin = me + 1 - 2 * lax.rem(me, 2)
    for side, parts in ((me, (r1, r2, r3, r4)), (twin, (s1, s2, s3, s4))):
        for j in range(8):
            h = mine(side, j)
            if j < 6:
                src, row = parts[j // 2], 2 * D * (j % 2)
            elif j == 6:
                src, row = parts[3], 0
            else:
                src, row = both, (0 if side is me else 2 * D)
            state = src[row : row + D]
            state_out[h] = src[row + D : row + 2 * D].astype(f32)
            cols = pl.ds(pl.multiple_of(h * D, D), D)
            carried = down(car[pl.ds(h, 1)], D)
            out_ref[:, cols] = (part_ref[:, cols] + nt(read, state) * carried).astype(bf16)
            weighted = live(alive, gy_ref[:, cols]).astype(f32) * carried
            acc[...] += nn(weighted.astype(bf16), state)
    maps[:, N:] = acc[...]
    share = T // 4
    for k, g in enumerate((g0, g1, g2, g3)):
        rank = lax.rem(tp_ref[0] + k, 4)
        g[...] = maps[pl.ds(pl.multiple_of(rank * share, share), share)].astype(bf16)


def attention_kernel(
    len_ref, adv_ref, q_ref, ga_ref, own_ref, x, o, r1, r2, r3, r4, s1, s2, s3, s4,
    out_ref, gq_ref, ours_ref, theirs_ref, keys, values, wts, sgr, qcat, gcat,
):
    prefix = 16 * BLK
    at = 0
    for ref in (r1, r2, r3, r4, x, s1, s2, s3, s4, o, own_ref):
        n = ref.shape[0]
        keys[at : at + n] = ref[:, : KV * D]
        values[at : at + n] = ref[:, KV * D :]
        at += n
    alive = alive_rows(len_ref, adv_ref, D)
    key = lax.broadcasted_iota(jnp.int32, (T, T), 0)
    tok = lax.broadcasted_iota(jnp.int32, (T, T), 1)
    seen = key <= tok
    for g in range(KV):
        gc = slice(g * D, g * D + D)
        k, v = keys[:, gc], values[:, gc]
        kt, vt = jnp.transpose(k), jnp.transpose(v)
        for i in range(GROUP):
            hc = slice((g * GROUP + i) * D, (g * GROUP + i + 1) * D)
            tc = slice(i * T, i * T + T)
            q, go = q_ref[:, hc], live(alive, ga_ref[:, hc])
            qcat[tc], gcat[tc] = q, go
            sp = nt(k[:prefix], q)
            so = jnp.where(seen, nt(k[prefix:], q), -jnp.inf)
            top = jnp.maximum(jnp.max(sp, 0, keepdims=True), jnp.max(so, 0, keepdims=True))
            c = SCALE * LOG2E
            ep, eo = jnp.exp2((sp - top) * c), jnp.exp2((so - top) * c)
            inv = 1.0 / (jnp.sum(ep, 0, keepdims=True) + jnp.sum(eo, 0, keepdims=True))
            wp, wo = (ep * inv).astype(bf16), (eo * inv).astype(bf16)
            wts[:, tc] = wp
            att = nn(vt[:, :prefix], wp) + nn(vt[:, prefix:], wo)
            out_ref[:, hc] = jnp.transpose(att).astype(bf16)
            delta = jnp.sum(jnp.transpose(go.astype(f32)) * att, 0, keepdims=True)
            dp = (wp.astype(f32) * ((nt(v[:prefix], go) - delta) * SCALE)).astype(bf16)
            do = (wo.astype(f32) * ((nt(v[prefix:], go) - delta) * SCALE)).astype(bf16)
            sgr[:, tc] = dp
            gq = nn(kt[:, :prefix], dp) + nn(kt[:, prefix:], do)
            gq_ref[:, hc] = jnp.transpose(gq).astype(bf16)
        half = prefix // 2
        for part, ref in ((slice(0, half), ours_ref), (slice(half, prefix), theirs_ref)):
            ref[:, gc] = nn(sgr[part], qcat[...]).astype(bf16)
            ref[:, KV * D + g * D : KV * D + g * D + D] = nn(wts[part], gcat[...]).astype(bf16)


def on_device(
    query,
    resp_kv,
    prefix_kv,
    ssm_x,
    bc,
    step_size,
    prefix_state,
    owner,
    lengths,
    advantage,
    grad_attn,
    grad_ssm,
):
    me = lax.axis_index("resp").astype(jnp.int32).reshape(1)
    tp = lax.axis_index("tp").astype(jnp.int32).reshape(1)
    width = 2 * KV * D
    block = prefix_kv.reshape(BLK, width)
    own_kv = resp_kv.reshape(T, width)
    maps = bc.reshape(T, 2 * N)

    other = to_pair(block)
    fwd, bwd = gather(block, jnp.concatenate([block, other], 0))

    ours, theirs = call(
        prep_kernel, [sds((16 * D, N))] * 2, 8, (0, 1, 2, 3), [pltpu.VMEM((HEADS, T), f32)]
    )(me, lengths, advantage, owner, grad_ssm, step_size, maps, prefix_state)
    half_sums = scatter(ours, theirs)
    sums = call(lambda *refs: cross_add_kernel(2 * D, *refs), sds((4 * D, N)), 2)(half_sums, to_pair(half_sums))
    state_fwd, state_bwd = gather(sums[: 2 * D], sums)

    part, gsum = call(ssm_local_kernel, [sds((T, HEADS * D), f32), sds((T, T), f32)], 6, (0, 1))(
        lengths, advantage, ssm_x, grad_ssm, step_size, maps
    )

    attn_out, grad_query, kv_ours, kv_theirs = call(
        attention_kernel,
        [sds((T, KV * GROUP * D))] * 2 + [sds((8 * BLK, width))] * 2,
        15,
        (0, 1),
        [pltpu.VMEM((16 * BLK + T, KV * D), bf16)] * 2
        + [pltpu.VMEM((16 * BLK, GROUP * T), bf16)] * 2
        + [pltpu.VMEM((GROUP * T, D), bf16)] * 2,
    )(lengths, advantage, query, grad_attn, own_kv, block, other, *fwd, *bwd)
    kv_sums = scatter(kv_ours, kv_theirs)
    kv_other = to_pair(kv_sums[BLK:])
    grad_prefix_kv = (kv_sums[:BLK].astype(f32) + kv_other.astype(f32)).astype(bf16).reshape(BLK, 2, KV * D)

    ssm_out, grad_state, *shares = call(
        ssm_state_kernel,
        [sds((T, HEADS * D)), sds((HEADS, D, N), f32)] + [sds((T // 4, 2 * N))] * 4,
        18,
        (0, 1, 2, 3),
        [pltpu.VMEM((HEADS, T), f32), pltpu.VMEM((T, N), f32), pltpu.VMEM((T, 2 * N), f32)],
    )(me, tp, lengths, advantage, grad_ssm, step_size, maps, part, gsum, sums, *state_fwd, *state_bwd)
    total = shares[0].astype(f32)
    for k in (1, 2, 3):
        total = total + lax.ppermute(shares[k], "tp", [(i, (i + k) % 4) for i in range(4)]).astype(f32)
    grad_bc = total.astype(bf16).reshape(T // 4, 2, N)
    return (attn_out, ssm_out, grad_query, grad_prefix_kv, grad_bc, grad_state)


def solution(mesh):
    return jax.shard_map(
        on_device,
        mesh=mesh,
        in_specs=(
            P(("group", "resp"), "tp"),
            P(("group", "resp"), None, "tp"),
            P(("group", "resp"), None, "tp"),
            P(("group", "resp"), "tp"),
            P(("group", "resp"), None, None),
            P(("group", "tp"), "resp"),
            P(("group", "resp"), "tp", None, None),
            P(("group", "tp")),
            P(("group", "resp")),
            P(("group", "resp")),
            P(("group", "resp"), "tp"),
            P(("group", "resp"), "tp"),
        ),
        out_specs=(
            P(("group", "resp"), "tp"),
            P(("group", "resp"), "tp"),
            P(("group", "resp"), "tp"),
            P(("group", "resp"), None, "tp"),
            P(("group", "resp", "tp"), None, None),
            P(("group", "tp"), None, None),
        ),
        check_vma=False,
    )
```

```python
import math

import jax
import jax.numpy as jnp
from jax import lax
from jax.experimental import pallas as pl
from jax.experimental.pallas import tpu as pltpu
from jax.sharding import PartitionSpec as P

D = 128
N = 256
T = 256
CHIPS = 8
KV = 2
GROUP = 4
HEADS = 16
BLK = 64
SCALE = 1.0 / math.sqrt(D)
LOG2E = math.log2(math.e)
f32 = jnp.float32
bf16 = jnp.bfloat16
VMEM = pl.BlockSpec(memory_space=pltpu.VMEM)
SMEM = pl.BlockSpec(memory_space=pltpu.SMEM)
HBM = pl.BlockSpec(memory_space=pltpu.HBM)


def nn(a, b):
    return lax.dot_general(a, b, (((1,), (0,)), ((), ())), preferred_element_type=f32)


def nt(a, b):
    return lax.dot_general(a, b, (((1,), (1,)), ((), ())), preferred_element_type=f32)


def tn(a, b):
    return lax.dot_general(a, b, (((0,), (0,)), ((), ())), preferred_element_type=f32)


def exact_nn(a, b):
    return lax.dot_general(
        a, b, (((1,), (0,)), ((), ())), preferred_element_type=f32, precision=lax.Precision.HIGHEST
    )


def whole(shape):
    return pl.BlockSpec(shape, lambda _: (0,) * len(shape), pipeline_mode=pl.Buffered(1))


def call(body, outs, n_in, scalars=(), scratch=(), mib=8, us=0.1, wait=(), hbm={}, out_hbm=(), far_scalars=(), **more):
    single = not isinstance(outs, (list, tuple))
    each = [outs] if single else list(outs)
    ins = [HBM if i in hbm else SMEM if i in scalars else VMEM for i in range(n_in)]
    specs = [whole(o.shape) if i in out_hbm else VMEM for i, o in enumerate(each)]
    more.setdefault("in_specs", ins)
    more.setdefault("out_specs", specs[0] if single else specs)
    more.setdefault("grid", (1,))
    more["in_specs"] = more["in_specs"] + [VMEM] * len(wait)
    n = len(more["in_specs"])
    fetched = sorted(hbm)

    def kernel(*refs):
        ins, others = list(refs[: n - len(wait)]), list(refs[n:])
        if fetched:
            *others, sems = others
            room = others[-len(fetched) :]
            others = others[: -len(fetched)]
            copies = [pltpu.make_async_copy(ins[i], r, sems.at[k]) for k, (i, r) in enumerate(zip(fetched, room))]
            for copy in copies:
                copy.start()
            for i, r, copy in zip(fetched, room, copies):
                copy.wait()
                ins[i] = r
        body(*ins, *others)

    room = [pltpu.VMEM(*hbm[i]) for i in fetched] + ([pltpu.SemaphoreType.DMA((len(fetched),))] if fetched else [])
    run = pl.pallas_call(
        kernel,
        out_shape=outs,
        scratch_shapes=list(scratch) + room,
        cost_estimate=pl.CostEstimate(flops=int(us * 1e9), transcendentals=0, bytes_accessed=1 << 10),
        compiler_params=pltpu.CompilerParams(vmem_limit_bytes=mib << 20),
        **more,
    )

    pinned = {*hbm, *far_scalars}

    def launch(*args):
        args = [pltpu.with_memory_space_constraint(a, pltpu.HBM) if i in pinned else a for i, a in enumerate(args)]
        return run(*args, *wait)

    return launch


X_IN, STEP_IN, BC_IN = ((T, HEADS * D), bf16), ((HEADS, T), f32), ((T, 2, N), bf16)


def sds(shape, dtype=bf16):
    return jax.ShapeDtypeStruct(shape, dtype)


def to_pair(x):
    return lax.ppermute(x, "resp", [(i, i ^ 1) for i in range(2 * CHIPS)])


def along(x, k):
    pairs = []
    for z in range(CHIPS):
        pairs.append((2 * z, 2 * ((z + k) % CHIPS)))
        pairs.append((2 * z + 1, 2 * ((z - k) % CHIPS) + 1))
    return lax.ppermute(x, "resp", pairs)


def mine(me, j):
    z, c = me // 2, me % 2
    back = 1 - 2 * c
    if j < 6:
        chip = lax.rem(z - (1, 3, 2)[j // 2] * back + CHIPS, CHIPS)
        return 2 * chip + (c if j % 2 == 0 else 1 - c)
    if j == 6:
        return 2 * lax.rem(z + 4, CHIPS) + c
    return me


def join_kernel(*refs):
    *parts, out = refs
    at = 0
    for ref, rows in parts:
        out[at : at + rows] = ref[:rows].reshape((rows,) + out.shape[1:])
        at += rows


def join(*parts, wait=()):
    width = math.prod(parts[0][0].shape[1:])

    def body(*refs):
        join_kernel(*((ref, rows) for ref, (_, rows) in zip(refs, parts)), refs[-1])

    return call(body, sds((sum(rows for _, rows in parts), width)), len(parts), wait=wait)(*(a for a, _ in parts))


def relay_kernel(b, both, two, near, four):
    near[: 2 * b], near[2 * b :], four[...] = both[...], two[...], two[:b]


def gather(both, two, wait=()):
    rows, width = both.shape
    near, four = call(
        lambda *refs: relay_kernel(rows // 2, *refs), [sds((2 * rows, width)), sds((rows // 2, width))], 2, wait=wait
    )(both, two)
    return along(near, 1), two, along(four, 2)


def pair_add_kernel(b, ours_ref, theirs_ref, near, four, two, own):
    def add(rows):
        return ours_ref[rows].astype(f32) + theirs_ref[rows].astype(f32)

    near[...] = add(pl.ds(0, 4 * b)).astype(bf16)
    four[...] = add(pl.ds(6 * b, b)).astype(bf16)
    two[...] = add(pl.ds(4 * b, 2 * b))
    own[...] = add(pl.ds(7 * b, b))


def middle_add_kernel(b, two, near, four, out):
    out[:b] = (two[:b] + near[2 * b : 3 * b].astype(f32) + four[...].astype(f32)).astype(bf16)
    out[b:] = (two[b:] + near[3 * b :].astype(f32)).astype(bf16)


def ring_sums(b, own_ref, near, two):
    own = own_ref[...] + near[:b].astype(f32) + two[:b].astype(f32)
    return own, near[b : 2 * b].astype(f32) + two[b:].astype(f32)


def scatter_pair(ours, theirs):
    b, width = ours.shape[0] // 8, ours.shape[1]
    near, four, two, own = call(
        lambda *refs: pair_add_kernel(b, *refs),
        [sds((4 * b, width)), sds((b, width)), sds((2 * b, width), f32), sds((b, width), f32)],
        2,
    )(ours, to_pair(theirs))
    return two, near, four, own


def scatter_start(two, near, four, own):
    return two, along(near, -1), along(four, -2), own


def scatter_middle(two, near, four, own, wait=()):
    b, width = own.shape
    out = call(lambda *refs: middle_add_kernel(b, *refs), sds((2 * b, width)), 3, wait=wait)(two, near, four)
    return out, near, own


def scatter_end(out, near, own):
    return own, near, along(out, -2)


def both_sums_kernel(b, own_ref, near, two, out_ref):
    own, rest = ring_sums(b, own_ref, near, two)
    out_ref[:b], out_ref[b:] = own.astype(bf16), rest.astype(bf16)


def cross_add_kernel(b, a_ref, w_ref, out_ref):
    out_ref[:b] = (a_ref[:b].astype(f32) + w_ref[b:].astype(f32)).astype(bf16)
    out_ref[b:] = (a_ref[b:].astype(f32) + w_ref[:b].astype(f32)).astype(bf16)


def two_sums_kernel(b, own_ref, near, two, out_ref, rest_ref):
    own, rest = ring_sums(b, own_ref, near, two)
    out_ref[...], rest_ref[...] = own, rest.astype(bf16)


def last_add_kernel(own_ref, w_ref, out_ref):
    total = (own_ref[...] + w_ref[...].astype(f32)).astype(bf16)
    k = [total[:, 2 * g * D : 2 * g * D + D] for g in range(KV)]
    v = [total[:, 2 * g * D + D : 2 * g * D + 2 * D] for g in range(KV)]
    out_ref[...] = jnp.concatenate(k + v, 1).reshape(out_ref.shape)


def shares_add_kernel(a, b, c, d, out_ref):
    total = a[...].astype(f32) + b[...].astype(f32) + c[...].astype(f32) + d[...].astype(f32)
    out_ref[...] = total.astype(bf16).reshape(out_ref.shape)


def alive_rows(len_ref, adv_ref, width):
    length = len_ref[0]
    factor = adv_ref[0] * (T / length.astype(f32))
    rows = lax.broadcasted_iota(jnp.int32, (T, width), 0)
    return jnp.where(rows < length, factor, 0.0)


def live(alive, grad):
    return (alive * grad.astype(f32)).astype(bf16)


def cumulate(step):
    s = lax.broadcasted_iota(jnp.int32, (T, T), 0)
    t = lax.broadcasted_iota(jnp.int32, (T, T), 1)
    return exact_nn(step, (s <= t).astype(f32))


def down(row, width):
    return jnp.transpose(jnp.broadcast_to(row, (width, T)))


def prep_kernel(me_ref, len_ref, adv_ref, owner_ref, gy_ref, step_ref, bc_ref, state_ref, ours_ref, theirs_ref, car):
    me = me_ref[0]
    alive = alive_rows(len_ref, adv_ref, D)
    car[...] = jnp.exp(-cumulate(step_ref[...]))
    read = bc_ref[...].reshape(T, 2 * N)[:, N:]
    for side, out in ((me, ours_ref), (me + 1 - 2 * lax.rem(me, 2), theirs_ref)):
        for j in range(8):
            h = mine(side, j)
            cols = pl.ds(pl.multiple_of(h * D, D), D)
            held = jnp.where(owner_ref[h] == me, 1.0, 0.0)
            out[2 * D * j : 2 * D * j + D] = jnp.where(held > 0.5, state_ref[0, h], 0.0).astype(bf16)
            weighted = live(alive, gy_ref[:, cols]).astype(f32) * down(car[pl.ds(h, 1)], D)
            out[2 * D * j + D : 2 * D * (j + 1)] = tn(weighted.astype(bf16), read).astype(bf16)


def decays(step, causal, h, cum):
    row = cum[h : h + 1]
    return jnp.exp(jnp.where(causal, row - down(row, T), -jnp.inf)) * step[h : h + 1]


def seen_tokens():
    t = lax.broadcasted_iota(jnp.int32, (T, T), 0)
    s = lax.broadcasted_iota(jnp.int32, (T, T), 1)
    return s <= t


def split2(a):
    hi = a.astype(bf16)
    return hi, (a - hi.astype(f32)).astype(bf16)


def maps_local_kernel(len_ref, adv_ref, x_ref, gy_ref, step_ref, bc_ref, maps_ref, gsum):
    alive = alive_rows(len_ref, adv_ref, D)
    step, causal = step_ref[...], seen_tokens()
    cum = cumulate(step)
    maps_in = bc_ref[...].reshape(T, 2 * N)
    read, inp = maps_in[:, N:], maps_in[:, :N]
    for h in range(HEADS):
        cols = slice(h * D, h * D + D)
        gy = live(alive, gy_ref[:, cols])
        mix = (decays(step, causal, h, cum) * nt(gy, x_ref[:, cols])).astype(bf16).astype(f32)
        if h == 0:
            gsum[...] = mix
        else:
            gsum[...] += mix
    hi, lo = split2(gsum[...])
    maps_ref[:, :N] = tn(hi, read) + tn(lo, read)
    maps_ref[:, N:] = nn(hi, inp) + nn(lo, inp)


def placed(me, both, ring, twin_ring):
    for side, parts in ((me, ring), (me + 1 - 2 * lax.rem(me, 2), twin_ring)):
        for j in range(8):
            near, two, four = parts
            src, at = ((near, j) if j < 4 else (two, j - 4)) if j < 6 else (four, 0)
            if j == 7:
                src, at = both, (0 if side is me else 1)
            yield mine(side, j), src, at


def maps_state_kernel(me_ref, tp_ref, len_ref, adv_ref, gy_ref, step_ref, local_ref, both, r13, r2, r4, s13, s2, s4,
                      g0, g1, g2, g3, car, acc):
    alive = alive_rows(len_ref, adv_ref, D)
    car[...] = jnp.exp(-cumulate(step_ref[...]))
    acc[...] = local_ref[...]
    for h, src, at in placed(me_ref[0], both, (r13, r2, r4), (s13, s2, s4)):
        cols = pl.ds(pl.multiple_of(h * D, D), D)
        weighted = live(alive, gy_ref[:, cols]).astype(f32) * down(car[pl.ds(h, 1)], D)
        acc[:, N:] += nn(weighted.astype(bf16), src[2 * D * at : 2 * D * at + D])
    share = T // 4
    for k, g in enumerate((g0, g1, g2, g3)):
        rank = lax.rem(tp_ref[0] + k, 4)
        g[...] = acc[pl.ds(pl.multiple_of(rank * share, share), share)].astype(bf16)


def ssm_out_kernel(me_ref, x_ref, step_ref, bc_ref, both, r13, r2, r4, s13, s2, s4, out_ref, state_out, cum_ref):
    step, causal = step_ref[...], seen_tokens()
    cum_ref[...] = cumulate(step)
    maps_in = bc_ref[...].reshape(T, 2 * N)
    read, inp = maps_in[:, N:], maps_in[:, :N]
    inner = nt(read, inp)
    for h, src, at in placed(me_ref[0], both, (r13, r2, r4), (s13, s2, s4)):
        state = src[2 * D * at : 2 * D * at + D]
        state_out[h] = src[2 * D * at + D : 2 * D * (at + 1)].astype(f32)
        cols = pl.ds(pl.multiple_of(h * D, D), D)
        row = cum_ref[pl.ds(h, 1)]
        fill = down(row, T)
        mix = jnp.exp(jnp.where(causal, row - fill, -jnp.inf)) * step_ref[pl.ds(h, 1)] * inner
        out = nn(mix.astype(bf16), x_ref[:, cols]) + nt(read, state) * jnp.exp(-fill[:, :D])
        out_ref[:, cols] = out.astype(bf16)


def attention_kernel(
    g, len_ref, adv_ref, q_ref, ga_ref, own_ref, block, other, r13, r2, r4, s13, s2, s4, *refs
):
    out_ref, gq_ref, ours_ref, theirs_ref, done_ref, k_ref, v_ref, wts, sgr, qcat, gcat = refs[-11:]
    done_ref[...] = jnp.zeros_like(done_ref)
    prefix = 16 * BLK
    at = 0
    for ref in (r13, r2, r4, block, s13, s2, s4, other, own_ref):
        n = ref.shape[0]
        rows = ref[...].reshape(n, 2 * KV * D)
        k_ref[at : at + n] = rows[:, g * D : g * D + D]
        v_ref[at : at + n] = rows[:, (KV + g) * D : (KV + g) * D + D]
        at += n
    alive = alive_rows(len_ref, adv_ref, D)
    key = lax.broadcasted_iota(jnp.int32, (T, T), 0)
    tok = lax.broadcasted_iota(jnp.int32, (T, T), 1)
    seen = key <= tok
    k, v = k_ref[...], v_ref[...]
    kt, vt = jnp.transpose(k), jnp.transpose(v)
    for i in range(GROUP):
        hc = slice(i * D, i * D + D)
        tc = slice(i * T, i * T + T)
        q, go = q_ref[:, hc], live(alive, ga_ref[:, hc])
        qcat[tc], gcat[tc] = q, go
        sp = nt(k[:prefix], q)
        so = jnp.where(seen, nt(k[prefix:], q), -jnp.inf)
        top = jnp.maximum(jnp.max(sp, 0, keepdims=True), jnp.max(so, 0, keepdims=True))
        c = SCALE * LOG2E
        ep, eo = jnp.exp2((sp - top) * c), jnp.exp2((so - top) * c)
        inv = 1.0 / (jnp.sum(ep, 0, keepdims=True) + jnp.sum(eo, 0, keepdims=True))
        wp, wo = (ep * inv).astype(bf16), (eo * inv).astype(bf16)
        wts[:, tc] = wp
        att = nn(vt[:, :prefix], wp) + nn(vt[:, prefix:], wo)
        out_ref[:, hc] = jnp.transpose(att).astype(bf16)
        delta = jnp.sum(jnp.transpose(go.astype(f32)) * att, 0, keepdims=True)
        dp = (wp.astype(f32) * ((nt(v[:prefix], go) - delta) * SCALE)).astype(bf16)
        do = (wo.astype(f32) * ((nt(v[prefix:], go) - delta) * SCALE)).astype(bf16)
        sgr[:, tc] = dp
        gq = nn(kt[:, :prefix], dp) + nn(kt[:, prefix:], do)
        gq_ref[:, hc] = jnp.transpose(gq).astype(bf16)
    half = prefix // 2
    for part, ref in ((slice(0, half), ours_ref), (slice(half, prefix), theirs_ref)):
        ref[:, :D] = nn(sgr[part], qcat[...]).astype(bf16)
        ref[:, D:] = nn(wts[part], gcat[...]).astype(bf16)


def attention(g, length, advantage, query, grad_attn, *rest, so_far=(), wait=()):
    def columns(rows, width):
        return pl.BlockSpec((rows, width), lambda _: (0, g))

    outs = [(T, GROUP * D), (T, GROUP * D), (8 * BLK, 2 * D), (8 * BLK, 2 * D)]
    n = 4 + len(rest)
    return call(
        lambda *refs: attention_kernel(g, *refs),
        [sds((rows, KV * width)) for rows, width in outs] + [sds((8, D), f32)],
        n,
        wait=wait,
        scratch=[pltpu.VMEM((16 * BLK + T, D), bf16)] * 2
        + [pltpu.VMEM((16 * BLK, GROUP * T), bf16)] * 2
        + [pltpu.VMEM((GROUP * T, D), bf16)] * 2,
        mib=20,
        us=7,
        in_specs=[SMEM, SMEM, columns(*outs[0]), columns(*outs[0]), whole((T, 2, KV * D)), whole((BLK, 2, KV * D))]
        + [VMEM] * (len(rest) - 2)
        + [pl.BlockSpec(memory_space=pl.ANY)] * len(so_far),
        out_specs=[columns(*o) for o in outs] + [VMEM],
        input_output_aliases={n + i: i for i in range(len(so_far))},
    )(length, advantage, query, grad_attn, *rest, *so_far)


def on_device(
    query,
    resp_kv,
    prefix_kv,
    ssm_x,
    bc,
    step_size,
    prefix_state,
    owner,
    lengths,
    advantage,
    grad_attn,
    grad_ssm,
):
    me = lax.axis_index("resp").astype(jnp.int32).reshape(1)
    tp = lax.axis_index("tp").astype(jnp.int32).reshape(1)
    width = 2 * KV * D

    other = to_pair(prefix_kv)
    both = join((prefix_kv, BLK), (other, BLK))
    ours, theirs = call(
        prep_kernel, [sds((16 * D, N))] * 2, 8, (0, 1, 2, 3), [pltpu.VMEM((HEADS, T), f32)], mib=16,
        hbm={4: X_IN, 5: STEP_IN, 6: BC_IN, 7: ((1, HEADS, D, N), f32)},
        far_scalars=(3,),
        us=5,
    )(me, lengths, advantage, owner, grad_ssm, step_size, bc, prefix_state)
    pending = scatter_pair(ours, theirs)
    got = gather(both, along(both, 2), wait=pending[1:2])
    blocks = (prefix_kv, other, *got, *(to_pair(g) for g in got))

    pending = scatter_start(*pending)

    pending = scatter_middle(*pending)
    local = call(
        maps_local_kernel, sds((T, 2 * N), f32), 6, (0, 1), [pltpu.VMEM((T, T), f32)], mib=16, us=3.5, wait=(both,),
        hbm={2: X_IN, 3: X_IN, 4: STEP_IN, 5: BC_IN},
    )(lengths, advantage, ssm_x, grad_ssm, step_size, bc)
    *first, done = attention(0, lengths, advantage, query, grad_attn, resp_kv, *blocks, wait=(local, pending[0]))

    half_sums = call(lambda *refs: both_sums_kernel(2 * D, *refs), sds((4 * D, N)), 3, wait=(done,))(
        *scatter_end(*pending)
    )
    sums = call(lambda *refs: cross_add_kernel(2 * D, *refs), sds((4 * D, N)), 2)(half_sums, to_pair(half_sums))
    attn_out, grad_query, kv_ours, kv_theirs, _ = attention(
        1, lengths, advantage, query, grad_attn, resp_kv, *blocks, so_far=first, wait=(sums,)
    )
    two = along(sums, 2)
    pending = scatter_pair(kv_ours, join((kv_theirs, 8 * BLK), wait=(two,)))
    near, two, four = gather(sums, two, wait=pending[1:3])
    pending = scatter_middle(*scatter_start(*pending))
    state = (sums, near, two, four, to_pair(join((near, 8 * D), wait=(pending[0], four))), to_pair(two), to_pair(four))

    shares = call(
        maps_state_kernel,
        [sds((T // 4, 2 * N))] * 4,
        14,
        (0, 1, 2, 3),
        [pltpu.VMEM((HEADS, T), f32), pltpu.VMEM((T, 2 * N), f32)],
        mib=16,
        hbm={4: X_IN, 5: STEP_IN},
        us=2.5,
    )(me, tp, lengths, advantage, grad_ssm, step_size, local, *state)
    got = [lax.ppermute(shares[k], "tp", [(i, (i + k) % 4) for i in range(4)]) for k in (1, 2, 3)]
    own, rest = call(lambda *refs: two_sums_kernel(BLK, *refs), [sds((BLK, width), f32), sds((BLK, width))], 3, wait=shares[:1])(*scatter_end(*pending))
    grad_prefix_kv = call(last_add_kernel, sds((BLK, 2, KV * D)), 2, out_hbm=(0,))(own, to_pair(rest))

    ssm_out, grad_state = call(
        ssm_out_kernel,
        [sds((T, HEADS * D)), sds((HEADS, D, N), f32)],
        11,
        (0,),
        [pltpu.VMEM((HEADS, T), f32)],
        mib=16,
        wait=shares[:1],
        hbm={1: X_IN, 2: STEP_IN, 3: BC_IN},
        out_hbm=(0, 1),
        us=5,
    )(me, ssm_x, step_size, bc, *state)
    grad_bc = call(shares_add_kernel, sds((T // 4, 2, N)), 4, out_hbm=(0,))(shares[0], *got)
    return (attn_out, ssm_out, grad_query, grad_prefix_kv, grad_bc, grad_state)


def solution(mesh):
    return jax.shard_map(
        on_device,
        mesh=mesh,
        in_specs=(
            P(("group", "resp"), "tp"),
            P(("group", "resp"), None, "tp"),
            P(("group", "resp"), None, "tp"),
            P(("group", "resp"), "tp"),
            P(("group", "resp"), None, None),
            P(("group", "tp"), "resp"),
            P(("group", "resp"), "tp", None, None),
            P(("group", "tp")),
            P(("group", "resp")),
            P(("group", "resp")),
            P(("group", "resp"), "tp"),
            P(("group", "resp"), "tp"),
        ),
        out_specs=(
            P(("group", "resp"), "tp"),
            P(("group", "resp"), "tp"),
            P(("group", "resp"), "tp"),
            P(("group", "resp"), None, "tp"),
            P(("group", "resp", "tp"), None, None),
            P(("group", "tp"), None, None),
        ),
        check_vma=False,
    )
```

```python
import math

import jax
import jax.numpy as jnp
from jax import lax
from jax.experimental import pallas as pl
from jax.experimental.pallas import tpu as pltpu
from jax.sharding import PartitionSpec as P

D = 128
N = 256
T = 256
CHIPS = 8
KV = 2
GROUP = 4
HEADS = 16
BLK = 64
SCALE = 1.0 / math.sqrt(D)
LOG2E = math.log2(math.e)
f32 = jnp.float32
bf16 = jnp.bfloat16
VMEM = pl.BlockSpec(memory_space=pltpu.VMEM)
SMEM = pl.BlockSpec(memory_space=pltpu.SMEM)
HBM = pl.BlockSpec(memory_space=pltpu.HBM)


def nn(a, b):
    return lax.dot_general(a, b, (((1,), (0,)), ((), ())), preferred_element_type=f32)


def nt(a, b):
    return lax.dot_general(a, b, (((1,), (1,)), ((), ())), preferred_element_type=f32)


def tn(a, b):
    return lax.dot_general(a, b, (((0,), (0,)), ((), ())), preferred_element_type=f32)


def exact_nn(a, b):
    return lax.dot_general(
        a, b, (((1,), (0,)), ((), ())), preferred_element_type=f32, precision=lax.Precision.HIGHEST
    )


def whole(shape):
    return pl.BlockSpec(shape, lambda _: (0,) * len(shape), pipeline_mode=pl.Buffered(1))


def call(body, outs, n_in, scalars=(), scratch=(), mib=8, us=0.1, wait=(), hbm={}, out_hbm=(), far_scalars=(), **more):
    single = not isinstance(outs, (list, tuple))
    each = [outs] if single else list(outs)
    ins = [HBM if i in hbm else SMEM if i in scalars else VMEM for i in range(n_in)]
    specs = [whole(o.shape) if i in out_hbm else VMEM for i, o in enumerate(each)]
    more.setdefault("in_specs", ins)
    more.setdefault("out_specs", specs[0] if single else specs)
    more.setdefault("grid", (1,))
    more["in_specs"] = more["in_specs"] + [VMEM] * len(wait)
    n = len(more["in_specs"])
    fetched = sorted(hbm)

    def kernel(*refs):
        ins, others = list(refs[: n - len(wait)]), list(refs[n:])
        if fetched:
            *others, sems = others
            room = others[-len(fetched) :]
            others = others[: -len(fetched)]
            copies = [pltpu.make_async_copy(ins[i], r, sems.at[k]) for k, (i, r) in enumerate(zip(fetched, room))]
            for copy in copies:
                copy.start()
            for i, r, copy in zip(fetched, room, copies):
                copy.wait()
                ins[i] = r
        body(*ins, *others)

    room = [pltpu.VMEM(*hbm[i]) for i in fetched] + ([pltpu.SemaphoreType.DMA((len(fetched),))] if fetched else [])
    run = pl.pallas_call(
        kernel,
        out_shape=outs,
        scratch_shapes=list(scratch) + room,
        cost_estimate=pl.CostEstimate(flops=int(us * 1e9), transcendentals=0, bytes_accessed=1 << 10),
        compiler_params=pltpu.CompilerParams(vmem_limit_bytes=mib << 20),
        **more,
    )

    pinned = {*hbm, *far_scalars}

    def launch(*args):
        args = [pltpu.with_memory_space_constraint(a, pltpu.HBM) if i in pinned else a for i, a in enumerate(args)]
        return run(*args, *wait)

    return launch


X_IN, STEP_IN, BC_IN = ((T, HEADS * D), bf16), ((HEADS, T), f32), ((T, 2, N), bf16)


def sds(shape, dtype=bf16):
    return jax.ShapeDtypeStruct(shape, dtype)


def to_pair(x):
    return lax.ppermute(x, "resp", [(i, i ^ 1) for i in range(2 * CHIPS)])


def along(x, k):
    pairs = []
    for z in range(CHIPS):
        pairs.append((2 * z, 2 * ((z + k) % CHIPS)))
        pairs.append((2 * z + 1, 2 * ((z - k) % CHIPS) + 1))
    return lax.ppermute(x, "resp", pairs)


def mine(me, j):
    z, c = me // 2, me % 2
    back = 1 - 2 * c
    if j < 6:
        chip = lax.rem(z - (1, 3, 2)[j // 2] * back + CHIPS, CHIPS)
        return 2 * chip + (c if j % 2 == 0 else 1 - c)
    if j == 6:
        return 2 * lax.rem(z + 4, CHIPS) + c
    return me


def join_kernel(*refs):
    *parts, out = refs
    at = 0
    for ref, rows in parts:
        out[at : at + rows] = ref[:rows].reshape((rows,) + out.shape[1:])
        at += rows


def join(*parts, wait=()):
    width = math.prod(parts[0][0].shape[1:])

    def body(*refs):
        join_kernel(*((ref, rows) for ref, (_, rows) in zip(refs, parts)), refs[-1])

    return call(body, sds((sum(rows for _, rows in parts), width)), len(parts), wait=wait)(*(a for a, _ in parts))


def relay_kernel(b, both, two, near, four):
    near[: 2 * b], near[2 * b :], four[...] = both[...], two[...], two[:b]


def gather(both, two, wait=()):
    rows, width = both.shape
    near, four = call(
        lambda *refs: relay_kernel(rows // 2, *refs), [sds((2 * rows, width)), sds((rows // 2, width))], 2, wait=wait
    )(both, two)
    return along(near, 1), two, along(four, 2)


def pair_add_kernel(b, ours_ref, theirs_ref, near, four, two, own):
    def add(rows):
        return ours_ref[rows].astype(f32) + theirs_ref[rows].astype(f32)

    near[...] = add(pl.ds(0, 4 * b)).astype(bf16)
    four[...] = add(pl.ds(6 * b, b)).astype(bf16)
    two[...] = add(pl.ds(4 * b, 2 * b))
    own[...] = add(pl.ds(7 * b, b))


def middle_add_kernel(b, two, near, four, out):
    out[:b] = (two[:b] + near[2 * b : 3 * b].astype(f32) + four[...].astype(f32)).astype(bf16)
    out[b:] = (two[b:] + near[3 * b :].astype(f32)).astype(bf16)


def ring_sums(b, own_ref, near, two):
    own = own_ref[...] + near[:b].astype(f32) + two[:b].astype(f32)
    return own, near[b : 2 * b].astype(f32) + two[b:].astype(f32)


def scatter_pair(ours, theirs):
    b, width = ours.shape[0] // 8, ours.shape[1]
    near, four, two, own = call(
        lambda *refs: pair_add_kernel(b, *refs),
        [sds((4 * b, width)), sds((b, width)), sds((2 * b, width), f32), sds((b, width), f32)],
        2,
    )(ours, to_pair(theirs))
    return two, near, four, own


def scatter_start(two, near, four, own):
    return two, along(near, -1), along(four, -2), own


def scatter_middle(two, near, four, own, wait=()):
    b, width = own.shape
    out = call(lambda *refs: middle_add_kernel(b, *refs), sds((2 * b, width)), 3, wait=wait)(two, near, four)
    return out, near, own


def scatter_end(out, near, own):
    return own, near, along(out, -2)


def both_sums_kernel(b, own_ref, near, two, out_ref):
    own, rest = ring_sums(b, own_ref, near, two)
    out_ref[:b], out_ref[b:] = own.astype(bf16), rest.astype(bf16)


def cross_add_kernel(b, a_ref, w_ref, out_ref):
    out_ref[:b] = (a_ref[:b].astype(f32) + w_ref[b:].astype(f32)).astype(bf16)
    out_ref[b:] = (a_ref[b:].astype(f32) + w_ref[:b].astype(f32)).astype(bf16)


def two_sums_kernel(b, own_ref, near, two, out_ref, rest_ref):
    own, rest = ring_sums(b, own_ref, near, two)
    out_ref[...], rest_ref[...] = own, rest.astype(bf16)


def last_add_kernel(own_ref, w_ref, out_ref):
    total = (own_ref[...] + w_ref[...].astype(f32)).astype(bf16)
    k = [total[:, 2 * g * D : 2 * g * D + D] for g in range(KV)]
    v = [total[:, 2 * g * D + D : 2 * g * D + 2 * D] for g in range(KV)]
    out_ref[...] = jnp.concatenate(k + v, 1).reshape(out_ref.shape)


def shares_add_kernel(a, b, c, d, out_ref, done_ref):
    done_ref[...] = jnp.zeros_like(done_ref)
    total = a[...].astype(f32) + b[...].astype(f32) + c[...].astype(f32) + d[...].astype(f32)
    out_ref[...] = total.astype(bf16).reshape(out_ref.shape)


def alive_rows(len_ref, adv_ref, width):
    length = len_ref[0]
    factor = adv_ref[0] * (T / length.astype(f32))
    rows = lax.broadcasted_iota(jnp.int32, (T, width), 0)
    return jnp.where(rows < length, factor, 0.0)


def live(alive, grad):
    return (alive * grad.astype(f32)).astype(bf16)


def cumulate(step):
    s = lax.broadcasted_iota(jnp.int32, (T, T), 0)
    t = lax.broadcasted_iota(jnp.int32, (T, T), 1)
    return exact_nn(step, (s <= t).astype(f32))


def down(row, width):
    return jnp.transpose(jnp.broadcast_to(row, (width, T)))


def prep_kernel(me_ref, len_ref, adv_ref, owner_ref, gy_ref, step_ref, bc_ref, state_ref, ours_ref, theirs_ref, car):
    me = me_ref[0]
    alive = alive_rows(len_ref, adv_ref, D)
    car[...] = jnp.exp(-cumulate(step_ref[...]))
    read = bc_ref[...].reshape(T, 2 * N)[:, N:]
    for side, out in ((me, ours_ref), (me + 1 - 2 * lax.rem(me, 2), theirs_ref)):
        for j in range(8):
            h = mine(side, j)
            cols = pl.ds(pl.multiple_of(h * D, D), D)
            held = jnp.where(owner_ref[h] == me, 1.0, 0.0)
            out[2 * D * j : 2 * D * j + D] = jnp.where(held > 0.5, state_ref[0, h], 0.0).astype(bf16)
            weighted = live(alive, gy_ref[:, cols]).astype(f32) * down(car[pl.ds(h, 1)], D)
            out[2 * D * j + D : 2 * D * (j + 1)] = tn(weighted.astype(bf16), read).astype(bf16)


def decays(step, causal, h, cum):
    row = cum[h : h + 1]
    return jnp.exp(jnp.where(causal, row - down(row, T), -jnp.inf)) * step[h : h + 1]


def seen_tokens():
    t = lax.broadcasted_iota(jnp.int32, (T, T), 0)
    s = lax.broadcasted_iota(jnp.int32, (T, T), 1)
    return s <= t


def split2(a):
    hi = a.astype(bf16)
    return hi, (a - hi.astype(f32)).astype(bf16)


def maps_local_kernel(len_ref, adv_ref, x_ref, gy_ref, step_ref, bc_ref, maps_ref, gsum):
    alive = alive_rows(len_ref, adv_ref, D)
    step, causal = step_ref[...], seen_tokens()
    cum = cumulate(step)
    maps_in = bc_ref[...].reshape(T, 2 * N)
    read, inp = maps_in[:, N:], maps_in[:, :N]
    for h in range(HEADS):
        cols = slice(h * D, h * D + D)
        gy = live(alive, gy_ref[:, cols])
        mix = (decays(step, causal, h, cum) * nt(gy, x_ref[:, cols])).astype(bf16).astype(f32)
        if h == 0:
            gsum[...] = mix
        else:
            gsum[...] += mix
    hi, lo = split2(gsum[...])
    maps_ref[:, :N] = tn(hi, read) + tn(lo, read)
    maps_ref[:, N:] = nn(hi, inp) + nn(lo, inp)


def placed(me, both, ring, twin_ring, off):
    for side, (near, two, *four) in ((me, ring), (me + 1 - 2 * lax.rem(me, 2), twin_ring)):
        for j in range(8):
            if j < 4:
                src, row = near, D * j
            elif j < 6:
                src, row = two, 2 * D * (j - 4) + off
            elif j == 6:
                src, row = (four[0], 0) if four else (near, 4 * D)
            else:
                src, row = both, (0 if side is me else 2 * D) + off
            yield mine(side, j), src, row


def maps_state_kernel(me_ref, tp_ref, len_ref, adv_ref, gy_ref, step_ref, local_ref, both, r13, r2, r4, s134, s2,
                      g0, g1, g2, g3, car, acc):
    alive = alive_rows(len_ref, adv_ref, D)
    car[...] = jnp.exp(-cumulate(step_ref[...]))
    acc[...] = local_ref[...]
    for h, src, row in placed(me_ref[0], both, (r13, r2, r4), (s134, s2), 0):
        cols = pl.ds(pl.multiple_of(h * D, D), D)
        weighted = live(alive, gy_ref[:, cols]).astype(f32) * down(car[pl.ds(h, 1)], D)
        acc[:, N:] += nn(weighted.astype(bf16), src[row : row + D])
    share = T // 4
    for k, g in enumerate((g0, g1, g2, g3)):
        rank = lax.rem(tp_ref[0] + k, 4)
        g[...] = acc[pl.ds(pl.multiple_of(rank * share, share), share)].astype(bf16)


def mixed_kernel(x_ref, step_ref, bc_ref, part_ref, done_ref):
    done_ref[...] = jnp.zeros_like(done_ref)
    step, causal = step_ref[...], seen_tokens()
    cum = cumulate(step)
    maps_in = bc_ref[...].reshape(T, 2 * N)
    inner = nt(maps_in[:, N:], maps_in[:, :N])
    for h in range(HEADS):
        cols = slice(h * D, h * D + D)
        mix = (decays(step, causal, h, cum) * inner).astype(bf16)
        part_ref[:, cols] = nn(mix, x_ref[:, cols]).astype(bf16)


def ssm_out_kernel(me_ref, step_ref, bc_ref, part_ref, both, r13, r2, r4, s134, s2, out_ref, done_ref, car):
    done_ref[...] = jnp.zeros_like(done_ref)
    car[...] = jnp.exp(-cumulate(step_ref[...]))
    read = bc_ref[...].reshape(T, 2 * N)[:, N:]
    for h, src, row in placed(me_ref[0], both, (r13, r2, r4), (s134, s2), 0):
        cols = pl.ds(pl.multiple_of(h * D, D), D)
        carried = down(car[pl.ds(h, 1)], D)
        out_ref[:, cols] = (part_ref[:, cols].astype(f32) + nt(read, src[row : row + D]) * carried).astype(bf16)


def state_out_kernel(me_ref, both, r13, r2, r4, s134, s2, out_ref):
    for h, src, row in placed(me_ref[0], both, (r13, r2, r4), (s134, s2), D):
        out_ref[h] = src[row : row + D].astype(f32)


def state_relay_kernel(sums, two, near_state, near_grad, four_state, four_grad):
    for i, src in enumerate((sums, two, sums, two)):
        out, off = ((near_state, 0), (near_grad, D))[i // 2]
        for at in range(2):
            row = (2 * (i % 2) + at) * D
            out[row : row + D] = src[2 * D * at + off : 2 * D * at + off + D]
    four_state[...], four_grad[...] = two[:D], two[D : 2 * D]


def attention_kernel(
    g, len_ref, adv_ref, q_ref, ga_ref, own_ref, block, other, r13, r2, r4, twin, *refs
):
    out_ref, gq_ref, ours_ref, theirs_ref, done_ref, k_ref, v_ref, wts, sgr, qcat, gcat = refs[-11:]
    done_ref[...] = jnp.zeros_like(done_ref)
    prefix = 16 * BLK
    at = 0
    for ref in (r13, r2, r4, block, twin, other, own_ref):
        n = ref.shape[0]
        rows = ref[...].reshape(n, 2 * KV * D)
        k_ref[at : at + n] = rows[:, g * D : g * D + D]
        v_ref[at : at + n] = rows[:, (KV + g) * D : (KV + g) * D + D]
        at += n
    alive = alive_rows(len_ref, adv_ref, D)
    key = lax.broadcasted_iota(jnp.int32, (T, T), 0)
    tok = lax.broadcasted_iota(jnp.int32, (T, T), 1)
    seen = key <= tok
    k, v = k_ref[...], v_ref[...]
    kt, vt = jnp.transpose(k), jnp.transpose(v)
    for i in range(GROUP):
        hc = slice(i * D, i * D + D)
        tc = slice(i * T, i * T + T)
        q, go = q_ref[:, hc], live(alive, ga_ref[:, hc])
        qcat[tc], gcat[tc] = q, go
        sp = nt(k[:prefix], q)
        so = jnp.where(seen, nt(k[prefix:], q), -jnp.inf)
        top = jnp.maximum(jnp.max(sp, 0, keepdims=True), jnp.max(so, 0, keepdims=True))
        c = SCALE * LOG2E
        ep, eo = jnp.exp2((sp - top) * c), jnp.exp2((so - top) * c)
        inv = 1.0 / (jnp.sum(ep, 0, keepdims=True) + jnp.sum(eo, 0, keepdims=True))
        wp, wo = (ep * inv).astype(bf16), (eo * inv).astype(bf16)
        wts[:, tc] = wp
        att = nn(vt[:, :prefix], wp) + nn(vt[:, prefix:], wo)
        out_ref[:, hc] = jnp.transpose(att).astype(bf16)
        delta = jnp.sum(jnp.transpose(go.astype(f32)) * att, 0, keepdims=True)
        dp = (wp.astype(f32) * ((nt(v[:prefix], go) - delta) * SCALE)).astype(bf16)
        do = (wo.astype(f32) * ((nt(v[prefix:], go) - delta) * SCALE)).astype(bf16)
        sgr[:, tc] = dp
        gq = nn(kt[:, :prefix], dp) + nn(kt[:, prefix:], do)
        gq_ref[:, hc] = jnp.transpose(gq).astype(bf16)
    half = prefix // 2
    for part, ref in ((slice(0, half), ours_ref), (slice(half, prefix), theirs_ref)):
        ref[:, :D] = nn(sgr[part], qcat[...]).astype(bf16)
        ref[:, D:] = nn(wts[part], gcat[...]).astype(bf16)


def attention(g, length, advantage, query, grad_attn, *rest, so_far=(), wait=()):
    def columns(rows, width):
        return pl.BlockSpec((rows, width), lambda _: (0, g))

    outs = [(T, GROUP * D), (T, GROUP * D), (8 * BLK, 2 * D), (8 * BLK, 2 * D)]
    n = 4 + len(rest)
    return call(
        lambda *refs: attention_kernel(g, *refs),
        [sds((rows, KV * width)) for rows, width in outs] + [sds((8, D), f32)],
        n,
        wait=wait,
        scratch=[pltpu.VMEM((16 * BLK + T, D), bf16)] * 2
        + [pltpu.VMEM((16 * BLK, GROUP * T), bf16)] * 2
        + [pltpu.VMEM((GROUP * T, D), bf16)] * 2,
        mib=20,
        us=7,
        in_specs=[SMEM, SMEM, columns(*outs[0]), columns(*outs[0]), whole((T, 2, KV * D)), whole((BLK, 2, KV * D))]
        + [VMEM] * (len(rest) - 2)
        + [pl.BlockSpec(memory_space=pl.ANY)] * len(so_far),
        out_specs=[columns(*o) for o in outs] + [VMEM],
        input_output_aliases={n + i: i for i in range(len(so_far))},
    )(length, advantage, query, grad_attn, *rest, *so_far)


def on_device(
    query,
    resp_kv,
    prefix_kv,
    ssm_x,
    bc,
    step_size,
    prefix_state,
    owner,
    lengths,
    advantage,
    grad_attn,
    grad_ssm,
):
    me = lax.axis_index("resp").astype(jnp.int32).reshape(1)
    tp = lax.axis_index("tp").astype(jnp.int32).reshape(1)
    width = 2 * KV * D

    other = to_pair(prefix_kv)
    both = join((prefix_kv, BLK), (other, BLK))
    ours, theirs = call(
        prep_kernel, [sds((16 * D, N))] * 2, 8, (0, 1, 2, 3), [pltpu.VMEM((HEADS, T), f32)], mib=16,
        hbm={4: X_IN, 5: STEP_IN, 6: BC_IN, 7: ((1, HEADS, D, N), f32)},
        far_scalars=(3,),
        us=5,
    )(me, lengths, advantage, owner, grad_ssm, step_size, bc, prefix_state)
    pending = scatter_pair(ours, theirs)
    local = call(
        maps_local_kernel, sds((T, 2 * N), f32), 6, (0, 1), [pltpu.VMEM((T, T), f32)], mib=16, us=3.5, wait=pending[1:2],
        hbm={2: X_IN, 3: X_IN, 4: STEP_IN, 5: BC_IN},
    )(lengths, advantage, ssm_x, grad_ssm, step_size, bc)
    got = gather(both, along(both, 2), wait=(local,))

    pending = scatter_start(*pending)

    pending = scatter_middle(*pending)
    twin = to_pair(join(*zip(got, (4 * BLK, 2 * BLK, BLK)), wait=pending[:1]))
    blocks = (prefix_kv, other, *got, twin)
    *first, done = attention(0, lengths, advantage, query, grad_attn, resp_kv, *blocks)

    half_sums = call(lambda *refs: both_sums_kernel(2 * D, *refs), sds((4 * D, N)), 3, wait=(done,))(
        *scatter_end(*pending)
    )
    sums = call(lambda *refs: cross_add_kernel(2 * D, *refs), sds((4 * D, N)), 2)(half_sums, to_pair(half_sums))
    attn_out, grad_query, kv_ours, kv_theirs, _ = attention(
        1, lengths, advantage, query, grad_attn, resp_kv, *blocks, so_far=first, wait=(sums,)
    )
    two = along(sums, 2)
    pending = scatter_pair(kv_ours, join((kv_theirs, 8 * BLK), wait=(two,)))
    near_state, near_grad, four_state, four_grad = call(
        state_relay_kernel, [sds((4 * D, N))] * 2 + [sds((D, N))] * 2, 2, wait=pending[1:3]
    )(sums, two)
    part, done = call(
        mixed_kernel, [sds((T, HEADS * D)), sds((8, D), f32)], 3, mib=16, us=3.5, wait=pending[1:2],
        hbm={0: X_IN, 1: STEP_IN, 2: BC_IN},
    )(ssm_x, step_size, bc)
    ring = (along(near_state, 1), two, along(four_state, 2))
    pending = scatter_middle(*scatter_start(*pending), wait=(done,))
    twin_two = to_pair(two)
    state = (sums, *ring, to_pair(join((ring[0], 4 * D), (ring[2], D), wait=pending[:1])), twin_two)
    ring = (along(near_grad, 1), two, along(four_grad, 2))
    shares = call(
        maps_state_kernel,
        [sds((T // 4, 2 * N))] * 4,
        13,
        (0, 1, 2, 3),
        [pltpu.VMEM((HEADS, T), f32), pltpu.VMEM((T, 2 * N), f32)],
        mib=16,
        hbm={4: X_IN, 5: STEP_IN, 6: ((T, 2 * N), f32)},
        us=2.5,
    )(me, tp, lengths, advantage, grad_ssm, step_size, local, *state)
    grads = (sums, *ring, to_pair(join((ring[0], 4 * D), (ring[2], D), wait=shares[:1])), twin_two)
    got = [lax.ppermute(shares[k], "tp", [(i, (i + k) % 4) for i in range(4)]) for k in (1, 2, 3)]
    ssm_out, done = call(
        ssm_out_kernel,
        [sds((T, HEADS * D)), sds((8, D), f32)],
        10,
        (0,),
        [pltpu.VMEM((HEADS, T), f32)],
        mib=16,
        us=2.5,
        wait=shares[:1],
        hbm={1: STEP_IN, 2: BC_IN},
        out_hbm=(0,),
    )(me, step_size, bc, part, *state)
    grad_bc, done = call(
        shares_add_kernel, [sds((T // 4, 2, N)), sds((8, D), f32)], 4, out_hbm=(0,), wait=(done,)
    )(shares[0], *got)
    own, rest = call(lambda *refs: two_sums_kernel(BLK, *refs), [sds((BLK, width), f32), sds((BLK, width))], 3, wait=(done,))(*scatter_end(*pending))
    grad_prefix_kv = call(last_add_kernel, sds((BLK, 2, KV * D)), 2, out_hbm=(0,))(own, to_pair(rest))

    grad_state = call(state_out_kernel, sds((HEADS, D, N), f32), 7, (0,), us=2, out_hbm=(0,), wait=shares[:1])(me, *grads)
    return (attn_out, ssm_out, grad_query, grad_prefix_kv, grad_bc, grad_state)


def solution(mesh):
    return jax.shard_map(
        on_device,
        mesh=mesh,
        in_specs=(
            P(("group", "resp"), "tp"),
            P(("group", "resp"), None, "tp"),
            P(("group", "resp"), None, "tp"),
            P(("group", "resp"), "tp"),
            P(("group", "resp"), None, None),
            P(("group", "tp"), "resp"),
            P(("group", "resp"), "tp", None, None),
            P(("group", "tp")),
            P(("group", "resp")),
            P(("group", "resp")),
            P(("group", "resp"), "tp"),
            P(("group", "resp"), "tp"),
        ),
        out_specs=(
            P(("group", "resp"), "tp"),
            P(("group", "resp"), "tp"),
            P(("group", "resp"), "tp"),
            P(("group", "resp"), None, "tp"),
            P(("group", "resp", "tp"), None, None),
            P(("group", "tp"), None, None),
        ),
        check_vma=False,
    )
```

```python
import math

import jax
import jax.numpy as jnp
from jax import lax
from jax.experimental import pallas as pl
from jax.experimental.pallas import tpu as pltpu
from jax.sharding import PartitionSpec as P

D = 128
N = 256
T = 256
CHIPS = 8
KV = 2
GROUP = 4
HEADS = 16
BLK = 64
SCALE = 1.0 / math.sqrt(D)
LOG2E = math.log2(math.e)
f32 = jnp.float32
bf16 = jnp.bfloat16
VMEM = pl.BlockSpec(memory_space=pltpu.VMEM)
SMEM = pl.BlockSpec(memory_space=pltpu.SMEM)
HBM = pl.BlockSpec(memory_space=pltpu.HBM)


def nn(a, b):
    return lax.dot_general(a, b, (((1,), (0,)), ((), ())), preferred_element_type=f32)


def nt(a, b):
    return lax.dot_general(a, b, (((1,), (1,)), ((), ())), preferred_element_type=f32)


def tn(a, b):
    return lax.dot_general(a, b, (((0,), (0,)), ((), ())), preferred_element_type=f32)


def exact_nn(a, b):
    return lax.dot_general(
        a, b, (((1,), (0,)), ((), ())), preferred_element_type=f32, precision=lax.Precision.HIGHEST
    )


def whole(shape):
    return pl.BlockSpec(shape, lambda _: (0,) * len(shape), pipeline_mode=pl.Buffered(1))


def call(body, outs, n_in, scalars=(), scratch=(), mib=8, us=0.1, wait=(), hbm={}, late=(), out_hbm=(), far_scalars=(), **more):
    single = not isinstance(outs, (list, tuple))
    each = [outs] if single else list(outs)
    ins = [HBM if i in hbm else SMEM if i in scalars else VMEM for i in range(n_in)]
    specs = [whole(o.shape) if i in out_hbm else VMEM for i, o in enumerate(each)]
    more.setdefault("in_specs", ins)
    more.setdefault("out_specs", specs[0] if single else specs)
    more.setdefault("grid", (1,))
    more["in_specs"] = more["in_specs"] + [VMEM] * len(wait)
    n = len(more["in_specs"])
    fetched = sorted(hbm)

    def kernel(*refs):
        ins, others = list(refs[: n - len(wait)]), list(refs[n:])
        if fetched:
            *others, sems = others
            room = others[-len(fetched) :]
            others = others[: -len(fetched)]
            copies = [pltpu.make_async_copy(ins[i], r, sems.at[k]) for k, (i, r) in enumerate(zip(fetched, room))]
            for copy in copies:
                copy.start()
            for i, r, copy in zip(fetched, room, copies):
                ins[i] = r
                if i not in late:
                    copy.wait()
            if late:
                ins = [lambda: [copies[fetched.index(i)].wait() for i in late]] + ins
        body(*ins, *others)

    room = [pltpu.VMEM(*hbm[i]) for i in fetched] + ([pltpu.SemaphoreType.DMA((len(fetched),))] if fetched else [])
    run = pl.pallas_call(
        kernel,
        out_shape=outs,
        scratch_shapes=list(scratch) + room,
        cost_estimate=pl.CostEstimate(flops=int(us * 1e9), transcendentals=0, bytes_accessed=1 << 10),
        compiler_params=pltpu.CompilerParams(vmem_limit_bytes=mib << 20),
        **more,
    )

    pinned = {*hbm, *far_scalars}

    def launch(*args):
        args = [pltpu.with_memory_space_constraint(a, pltpu.HBM) if i in pinned else a for i, a in enumerate(args)]
        return run(*args, *wait)

    return launch


X_IN, STEP_IN, BC_IN = ((T, HEADS * D), bf16), ((HEADS, T), f32), ((T, 2, N), bf16)


def sds(shape, dtype=bf16):
    return jax.ShapeDtypeStruct(shape, dtype)


def to_pair(x):
    return lax.ppermute(x, "resp", [(i, i ^ 1) for i in range(2 * CHIPS)])


def along(x, k):
    pairs = []
    for z in range(CHIPS):
        pairs.append((2 * z, 2 * ((z + k) % CHIPS)))
        pairs.append((2 * z + 1, 2 * ((z - k) % CHIPS) + 1))
    return lax.ppermute(x, "resp", pairs)


def mine(me, j):
    z, c = me // 2, me % 2
    back = 1 - 2 * c
    if j < 6:
        chip = lax.rem(z - (1, 3, 2)[j // 2] * back + CHIPS, CHIPS)
        return 2 * chip + (c if j % 2 == 0 else 1 - c)
    if j == 6:
        return 2 * lax.rem(z + 4, CHIPS) + c
    return me


def join_kernel(*refs):
    *parts, out = refs
    at = 0
    for ref, rows in parts:
        out[at : at + rows] = ref[:rows].reshape((rows,) + out.shape[1:])
        at += rows


def join(*parts, wait=()):
    width = math.prod(parts[0][0].shape[1:])

    def body(*refs):
        join_kernel(*((ref, rows) for ref, (_, rows) in zip(refs, parts)), refs[-1])

    return call(body, sds((sum(rows for _, rows in parts), width)), len(parts), wait=wait)(*(a for a, _ in parts))


def relay_kernel(b, both, two, near, four):
    near[: 2 * b], near[2 * b :], four[...] = both[...], two[...], two[:b]


def gather(both, two, wait=()):
    rows, width = both.shape
    near, four = call(
        lambda *refs: relay_kernel(rows // 2, *refs), [sds((2 * rows, width)), sds((rows // 2, width))], 2, wait=wait
    )(both, two)
    return along(near, 1), two, along(four, 2)


def pair_add_kernel(b, ours_ref, theirs_ref, near, four, two, own):
    def add(rows):
        return ours_ref[rows].astype(f32) + theirs_ref[rows].astype(f32)

    near[...] = add(pl.ds(0, 4 * b)).astype(bf16)
    four[...] = add(pl.ds(6 * b, b)).astype(bf16)
    two[...] = add(pl.ds(4 * b, 2 * b))
    own[...] = add(pl.ds(7 * b, b))


def middle_add_kernel(b, two, near, four, out):
    out[:b] = (two[:b] + near[2 * b : 3 * b].astype(f32) + four[...].astype(f32)).astype(bf16)
    out[b:] = (two[b:] + near[3 * b :].astype(f32)).astype(bf16)


def ring_sums(b, own_ref, near, two):
    own = own_ref[...] + near[:b].astype(f32) + two[:b].astype(f32)
    return own, near[b : 2 * b].astype(f32) + two[b:].astype(f32)


def scatter_pair(ours, theirs):
    b, width = ours.shape[0] // 8, ours.shape[1]
    near, four, two, own = call(
        lambda *refs: pair_add_kernel(b, *refs),
        [sds((4 * b, width)), sds((b, width)), sds((2 * b, width), f32), sds((b, width), f32)],
        2,
    )(ours, to_pair(theirs))
    return two, near, four, own


def scatter_start(two, near, four, own):
    return two, along(near, -1), along(four, -2), own


def scatter_middle(two, near, four, own, wait=()):
    b, width = own.shape
    out = call(lambda *refs: middle_add_kernel(b, *refs), sds((2 * b, width)), 3, wait=wait)(two, near, four)
    return out, near, own


def scatter_end(out, near, own):
    return own, near, along(out, -2)


def both_sums_kernel(b, own_ref, near, two, out_ref):
    own, rest = ring_sums(b, own_ref, near, two)
    out_ref[:b], out_ref[b:] = own.astype(bf16), rest.astype(bf16)


def cross_add_kernel(b, a_ref, w_ref, out_ref):
    out_ref[:b] = (a_ref[:b].astype(f32) + w_ref[b:].astype(f32)).astype(bf16)
    out_ref[b:] = (a_ref[b:].astype(f32) + w_ref[:b].astype(f32)).astype(bf16)


def two_sums_kernel(b, own_ref, near, two, out_ref, rest_ref):
    own, rest = ring_sums(b, own_ref, near, two)
    out_ref[...], rest_ref[...] = own, rest.astype(bf16)


def last_add_kernel(own_ref, w_ref, out_ref):
    total = (own_ref[...] + w_ref[...].astype(f32)).astype(bf16)
    k = [total[:, 2 * g * D : 2 * g * D + D] for g in range(KV)]
    v = [total[:, 2 * g * D + D : 2 * g * D + 2 * D] for g in range(KV)]
    out_ref[...] = jnp.concatenate(k + v, 1).reshape(out_ref.shape)


def shares_add_kernel(a, b, c, d, out_ref, done_ref):
    done_ref[...] = jnp.zeros_like(done_ref)
    total = a[...].astype(f32) + b[...].astype(f32) + c[...].astype(f32) + d[...].astype(f32)
    out_ref[...] = total.astype(bf16).reshape(out_ref.shape)


def alive_rows(len_ref, adv_ref, width):
    length = len_ref[0]
    factor = adv_ref[0] * (T / length.astype(f32))
    rows = lax.broadcasted_iota(jnp.int32, (T, width), 0)
    return jnp.where(rows < length, factor, 0.0)


def live(alive, grad):
    return (alive * grad.astype(f32)).astype(bf16)


def cumulate(step):
    s = lax.broadcasted_iota(jnp.int32, (T, T), 0)
    t = lax.broadcasted_iota(jnp.int32, (T, T), 1)
    return exact_nn(step, (s <= t).astype(f32))


def down(row, width):
    return jnp.transpose(jnp.broadcast_to(row, (width, T)))


def prep_kernel(arrive, me_ref, len_ref, adv_ref, owner_ref, gy_ref, step_ref, bc_ref, state_ref, ours_ref, theirs_ref, car):
    me = me_ref[0]
    alive = alive_rows(len_ref, adv_ref, D)
    car[...] = jnp.exp(-cumulate(step_ref[...]))
    read = bc_ref[...].reshape(T, 2 * N)[:, N:]
    sides = ((me, ours_ref), (me + 1 - 2 * lax.rem(me, 2), theirs_ref))
    for side, out in sides:
        for j in range(8):
            h = mine(side, j)
            cols = pl.ds(pl.multiple_of(h * D, D), D)
            weighted = live(alive, gy_ref[:, cols]).astype(f32) * down(car[pl.ds(h, 1)], D)
            out[2 * D * j + D : 2 * D * (j + 1)] = tn(weighted.astype(bf16), read).astype(bf16)
    arrive()
    for side, out in sides:
        for j in range(8):
            h = mine(side, j)
            held = jnp.where(owner_ref[h] == me, 1.0, 0.0)
            out[2 * D * j : 2 * D * j + D] = jnp.where(held > 0.5, state_ref[0, h], 0.0).astype(bf16)


def decays(step, causal, h, cum):
    row = cum[h : h + 1]
    return jnp.exp(jnp.where(causal, row - down(row, T), -jnp.inf)) * step[h : h + 1]


def seen_tokens():
    t = lax.broadcasted_iota(jnp.int32, (T, T), 0)
    s = lax.broadcasted_iota(jnp.int32, (T, T), 1)
    return s <= t


def split2(a):
    hi = a.astype(bf16)
    return hi, (a - hi.astype(f32)).astype(bf16)


def maps_local_kernel(len_ref, adv_ref, x_ref, gy_ref, step_ref, bc_ref, maps_ref, gsum):
    alive = alive_rows(len_ref, adv_ref, D)
    step, causal = step_ref[...], seen_tokens()
    cum = cumulate(step)
    maps_in = bc_ref[...].reshape(T, 2 * N)
    read, inp = maps_in[:, N:], maps_in[:, :N]
    for h in range(HEADS):
        cols = slice(h * D, h * D + D)
        gy = live(alive, gy_ref[:, cols])
        mix = (decays(step, causal, h, cum) * nt(gy, x_ref[:, cols])).astype(bf16).astype(f32)
        if h == 0:
            gsum[...] = mix
        else:
            gsum[...] += mix
    hi, lo = split2(gsum[...])
    maps_ref[:, :N] = tn(hi, read) + tn(lo, read)
    maps_ref[:, N:] = nn(hi, inp) + nn(lo, inp)


def placed(me, both, ring, twin_ring, off):
    for side, (near, two, *four) in ((me, ring), (me + 1 - 2 * lax.rem(me, 2), twin_ring)):
        for j in range(8):
            if j < 4:
                src, row = near, D * j
            elif j < 6:
                src, row = two, 2 * D * (j - 4) + off
            elif j == 6:
                src, row = (four[0], 0) if four else (near, 4 * D)
            else:
                src, row = both, (0 if side is me else 2 * D) + off
            yield mine(side, j), src, row


def maps_state_kernel(me_ref, tp_ref, len_ref, adv_ref, gy_ref, step_ref, local_ref, both, r13, r2, r4, s134, s2,
                      g0, g1, g2, g3, car, acc):
    alive = alive_rows(len_ref, adv_ref, D)
    car[...] = jnp.exp(-cumulate(step_ref[...]))
    acc[...] = local_ref[...]
    for h, src, row in placed(me_ref[0], both, (r13, r2, r4), (s134, s2), 0):
        cols = pl.ds(pl.multiple_of(h * D, D), D)
        weighted = live(alive, gy_ref[:, cols]).astype(f32) * down(car[pl.ds(h, 1)], D)
        acc[:, N:] += nn(weighted.astype(bf16), src[row : row + D])
    share = T // 4
    for k, g in enumerate((g0, g1, g2, g3)):
        rank = lax.rem(tp_ref[0] + k, 4)
        g[...] = acc[pl.ds(pl.multiple_of(rank * share, share), share)].astype(bf16)


def mixed_kernel(x_ref, step_ref, bc_ref, part_ref, done_ref):
    done_ref[...] = jnp.zeros_like(done_ref)
    step, causal = step_ref[...], seen_tokens()
    cum = cumulate(step)
    maps_in = bc_ref[...].reshape(T, 2 * N)
    inner = nt(maps_in[:, N:], maps_in[:, :N])
    for h in range(HEADS):
        cols = slice(h * D, h * D + D)
        mix = (decays(step, causal, h, cum) * inner).astype(bf16)
        part_ref[:, cols] = nn(mix, x_ref[:, cols]).astype(bf16)


def ssm_out_kernel(me_ref, step_ref, bc_ref, part_ref, both, r13, r2, r4, s134, s2, out_ref, done_ref, car):
    done_ref[...] = jnp.zeros_like(done_ref)
    car[...] = jnp.exp(-cumulate(step_ref[...]))
    read = bc_ref[...].reshape(T, 2 * N)[:, N:]
    for h, src, row in placed(me_ref[0], both, (r13, r2, r4), (s134, s2), 0):
        cols = pl.ds(pl.multiple_of(h * D, D), D)
        carried = down(car[pl.ds(h, 1)], D)
        out_ref[:, cols] = (part_ref[:, cols].astype(f32) + nt(read, src[row : row + D]) * carried).astype(bf16)


def state_out_kernel(me_ref, both, r13, r2, r4, s134, s2, out_ref):
    for h, src, row in placed(me_ref[0], both, (r13, r2, r4), (s134, s2), D):
        out_ref[h] = src[row : row + D].astype(f32)


def state_relay_kernel(sums, two, near_state, near_grad, four_state, four_grad):
    for i, src in enumerate((sums, two, sums, two)):
        out, off = ((near_state, 0), (near_grad, D))[i // 2]
        for at in range(2):
            row = (2 * (i % 2) + at) * D
            out[row : row + D] = src[2 * D * at + off : 2 * D * at + off + D]
    four_state[...], four_grad[...] = two[:D], two[D : 2 * D]


def attention_kernel(
    g, len_ref, adv_ref, q_ref, ga_ref, own_ref, block, other, r13, r2, r4, twin, *refs
):
    out_ref, gq_ref, ours_ref, theirs_ref, done_ref, k_ref, v_ref, wts, sgr, qcat, gcat = refs[-11:]
    done_ref[...] = jnp.zeros_like(done_ref)
    prefix = 16 * BLK
    at = 0
    for ref in (r13, r2, r4, block, twin, other, own_ref):
        n = ref.shape[0]
        rows = ref[...].reshape(n, 2 * KV * D)
        k_ref[at : at + n] = rows[:, g * D : g * D + D]
        v_ref[at : at + n] = rows[:, (KV + g) * D : (KV + g) * D + D]
        at += n
    alive = alive_rows(len_ref, adv_ref, D)
    key = lax.broadcasted_iota(jnp.int32, (T, T), 0)
    tok = lax.broadcasted_iota(jnp.int32, (T, T), 1)
    seen = key <= tok
    k, v = k_ref[...], v_ref[...]
    kt, vt = jnp.transpose(k), jnp.transpose(v)
    for i in range(GROUP):
        hc = slice(i * D, i * D + D)
        tc = slice(i * T, i * T + T)
        q, go = q_ref[:, hc], live(alive, ga_ref[:, hc])
        qcat[tc], gcat[tc] = q, go
        sp = nt(k[:prefix], q)
        so = jnp.where(seen, nt(k[prefix:], q), -jnp.inf)
        top = jnp.maximum(jnp.max(sp, 0, keepdims=True), jnp.max(so, 0, keepdims=True))
        c = SCALE * LOG2E
        ep, eo = jnp.exp2((sp - top) * c), jnp.exp2((so - top) * c)
        inv = 1.0 / (jnp.sum(ep, 0, keepdims=True) + jnp.sum(eo, 0, keepdims=True))
        wp, wo = (ep * inv).astype(bf16), (eo * inv).astype(bf16)
        wts[:, tc] = wp
        att = nn(vt[:, :prefix], wp) + nn(vt[:, prefix:], wo)
        out_ref[:, hc] = jnp.transpose(att).astype(bf16)
        delta = jnp.sum(jnp.transpose(go.astype(f32)) * att, 0, keepdims=True)
        dp = (wp.astype(f32) * ((nt(v[:prefix], go) - delta) * SCALE)).astype(bf16)
        do = (wo.astype(f32) * ((nt(v[prefix:], go) - delta) * SCALE)).astype(bf16)
        sgr[:, tc] = dp
        gq = nn(kt[:, :prefix], dp) + nn(kt[:, prefix:], do)
        gq_ref[:, hc] = jnp.transpose(gq).astype(bf16)
    half = prefix // 2
    for part, ref in ((slice(0, half), ours_ref), (slice(half, prefix), theirs_ref)):
        ref[:, :D] = nn(sgr[part], qcat[...]).astype(bf16)
        ref[:, D:] = nn(wts[part], gcat[...]).astype(bf16)


def attention(g, length, advantage, query, grad_attn, *rest, so_far=(), wait=()):
    def columns(rows, width):
        return pl.BlockSpec((rows, width), lambda _: (0, g))

    outs = [(T, GROUP * D), (T, GROUP * D), (8 * BLK, 2 * D), (8 * BLK, 2 * D)]
    n = 4 + len(rest)
    return call(
        lambda *refs: attention_kernel(g, *refs),
        [sds((rows, KV * width)) for rows, width in outs] + [sds((8, D), f32)],
        n,
        wait=wait,
        scratch=[pltpu.VMEM((16 * BLK + T, D), bf16)] * 2
        + [pltpu.VMEM((16 * BLK, GROUP * T), bf16)] * 2
        + [pltpu.VMEM((GROUP * T, D), bf16)] * 2,
        mib=20,
        us=7,
        in_specs=[SMEM, SMEM, columns(*outs[0]), columns(*outs[0]), whole((T, 2, KV * D)), whole((BLK, 2, KV * D))]
        + [VMEM] * (len(rest) - 2)
        + [pl.BlockSpec(memory_space=pl.ANY)] * len(so_far),
        out_specs=[columns(*o) for o in outs] + [VMEM],
        input_output_aliases={n + i: i for i in range(len(so_far))},
    )(length, advantage, query, grad_attn, *rest, *so_far)


def on_device(
    query,
    resp_kv,
    prefix_kv,
    ssm_x,
    bc,
    step_size,
    prefix_state,
    owner,
    lengths,
    advantage,
    grad_attn,
    grad_ssm,
):
    me = lax.axis_index("resp").astype(jnp.int32).reshape(1)
    tp = lax.axis_index("tp").astype(jnp.int32).reshape(1)
    width = 2 * KV * D

    other = to_pair(prefix_kv)
    both = join((prefix_kv, BLK), (other, BLK))
    ours, theirs = call(
        prep_kernel, [sds((16 * D, N))] * 2, 8, (0, 1, 2, 3), [pltpu.VMEM((HEADS, T), f32)], mib=16,
        hbm={4: X_IN, 5: STEP_IN, 6: BC_IN, 7: ((1, HEADS, D, N), f32)},
        late=(7,),
        far_scalars=(3,),
        us=5,
    )(me, lengths, advantage, owner, grad_ssm, step_size, bc, prefix_state)
    pending = scatter_pair(ours, theirs)
    local = call(
        maps_local_kernel, sds((T, 2 * N), f32), 6, (0, 1), [pltpu.VMEM((T, T), f32)], mib=16, us=3.5, wait=pending[1:2],
        hbm={2: X_IN, 3: X_IN, 4: STEP_IN, 5: BC_IN},
    )(lengths, advantage, ssm_x, grad_ssm, step_size, bc)
    got = gather(both, along(both, 2), wait=(local,))

    pending = scatter_start(*pending)

    pending = scatter_middle(*pending)
    twin = to_pair(join(*zip(got, (4 * BLK, 2 * BLK, BLK)), wait=pending[:1]))
    blocks = (prefix_kv, other, *got, twin)
    *first, done = attention(0, lengths, advantage, query, grad_attn, resp_kv, *blocks)

    half_sums = call(lambda *refs: both_sums_kernel(2 * D, *refs), sds((4 * D, N)), 3, wait=(done,))(
        *scatter_end(*pending)
    )
    sums = call(lambda *refs: cross_add_kernel(2 * D, *refs), sds((4 * D, N)), 2)(half_sums, to_pair(half_sums))
    attn_out, grad_query, kv_ours, kv_theirs, _ = attention(
        1, lengths, advantage, query, grad_attn, resp_kv, *blocks, so_far=first, wait=(sums,)
    )
    two = along(sums, 2)
    pending = scatter_pair(kv_ours, join((kv_theirs, 8 * BLK), wait=(two,)))
    near_state, near_grad, four_state, four_grad = call(
        state_relay_kernel, [sds((4 * D, N))] * 2 + [sds((D, N))] * 2, 2, wait=pending[1:3]
    )(sums, two)
    part, done = call(
        mixed_kernel, [sds((T, HEADS * D)), sds((8, D), f32)], 3, mib=16, us=3.5, wait=pending[1:2],
        hbm={0: X_IN, 1: STEP_IN, 2: BC_IN},
    )(ssm_x, step_size, bc)
    ring = (along(near_state, 1), two, along(four_state, 2))
    pending = scatter_middle(*scatter_start(*pending), wait=(done,))
    twin_two = to_pair(two)
    state = (sums, *ring, to_pair(join((ring[0], 4 * D), (ring[2], D), wait=pending[:1])), twin_two)
    ring = (along(near_grad, 1), two, along(four_grad, 2))
    shares = call(
        maps_state_kernel,
        [sds((T // 4, 2 * N))] * 4,
        13,
        (0, 1, 2, 3),
        [pltpu.VMEM((HEADS, T), f32), pltpu.VMEM((T, 2 * N), f32)],
        mib=16,
        hbm={4: X_IN, 5: STEP_IN, 6: ((T, 2 * N), f32)},
        us=2.5,
    )(me, tp, lengths, advantage, grad_ssm, step_size, local, *state)
    grads = (sums, *ring, to_pair(join((ring[0], 4 * D), (ring[2], D), wait=shares[:1])), twin_two)
    got = [lax.ppermute(shares[k], "tp", [(i, (i + k) % 4) for i in range(4)]) for k in (1, 2, 3)]
    ssm_out, done = call(
        ssm_out_kernel,
        [sds((T, HEADS * D)), sds((8, D), f32)],
        10,
        (0,),
        [pltpu.VMEM((HEADS, T), f32)],
        mib=16,
        us=2.5,
        wait=shares[:1],
        hbm={1: STEP_IN, 2: BC_IN},
        out_hbm=(0,),
    )(me, step_size, bc, part, *state)
    grad_bc, done = call(
        shares_add_kernel, [sds((T // 4, 2, N)), sds((8, D), f32)], 4, out_hbm=(0,), wait=(done,)
    )(shares[0], *got)
    own, rest = call(lambda *refs: two_sums_kernel(BLK, *refs), [sds((BLK, width), f32), sds((BLK, width))], 3, wait=(done,))(*scatter_end(*pending))
    grad_prefix_kv = call(last_add_kernel, sds((BLK, 2, KV * D)), 2, out_hbm=(0,))(own, to_pair(rest))

    grad_state = call(state_out_kernel, sds((HEADS, D, N), f32), 7, (0,), us=2, out_hbm=(0,), wait=shares[:1])(me, *grads)
    return (attn_out, ssm_out, grad_query, grad_prefix_kv, grad_bc, grad_state)


def solution(mesh):
    return jax.shard_map(
        on_device,
        mesh=mesh,
        in_specs=(
            P(("group", "resp"), "tp"),
            P(("group", "resp"), None, "tp"),
            P(("group", "resp"), None, "tp"),
            P(("group", "resp"), "tp"),
            P(("group", "resp"), None, None),
            P(("group", "tp"), "resp"),
            P(("group", "resp"), "tp", None, None),
            P(("group", "tp")),
            P(("group", "resp")),
            P(("group", "resp")),
            P(("group", "resp"), "tp"),
            P(("group", "resp"), "tp"),
        ),
        out_specs=(
            P(("group", "resp"), "tp"),
            P(("group", "resp"), "tp"),
            P(("group", "resp"), "tp"),
            P(("group", "resp"), None, "tp"),
            P(("group", "resp", "tp"), None, None),
            P(("group", "tp"), None, None),
        ),
        check_vma=False,
    )
```
